256 devices in a mesh: grp: 16 (over z_lo, x), own: 16 (over z_hi, y, core).
Axes of the slice: x: 4, y: 4, z: 8 (z_hi: 2, z_lo: 4; z = z_hi * 4 + z_lo), core: 2. Of those that a mesh axis runs over, the one named last changes fastest.
Arguments:
- vectors: float32 [16, 64, 2048], P('own'), may hold values from -6 to 6
- tiles: float32 [16, 16, 128, 128, 128], P('grp', 'own'), may hold values from -0.046875 to 0.046875
- tile_rows: int32 [16, 16, 128], P('grp', 'own'), may hold values from 0 to 15
- tile_cols: int32 [16, 16, 128], P('grp', 'own'), may hold values from 0 to 63
- tile_counts: int32 [16, 16], P('grp', 'own'), may hold values from 16 to 128, as said below
- matchings: int32 [16, 3], P('grp'), may hold values from 1 to 15, as said below
Outputs:
- products: float32 [16, 64, 2048], P('own', None, 'grp')
The draws below stay inside these ranges and needn't reach their ends.
Inputs may be any that keep to these rules, and one draw needn't show every extreme that they name: `tile_counts`: the largest value 128 is held by some device in every draw. Each row holds 3 different values; matching j of part g pairs owner o with owner o XOR matchings[g, j].
All inputs are finite; a program needn't handle non-finite values.
Results may differ from the reference program's by a relative error of at most 0.0003.
Values sent between devices are 32-bit elements; how exact they have to be, the bound alone decides.
No kernel may reach another device: no remote copies, remote signals or barrier semaphores. Data moves between devices by JAX's collectives and lax.ppermute only.
A program may use at most 64 MiB of HBM per device.

```python
import jax
import jax.numpy as jnp
from jax import lax

K = 64
TILE = 128
ROWS_OWN = 2048
MAX_TILES = 128
MATCH = 3
NBLK = 16
N_GRP = 16
N_OWN = 16


def draw_tile_counts(key, part):
    key_level, key_spot = jax.random.split(key)
    levels = jax.random.randint(key_level, (N_GRP * N_OWN,), 0, 4)
    counts = MAX_TILES // 8 * jnp.left_shift(jnp.ones_like(levels), levels)
    spot = jax.random.randint(key_spot, (), 0, N_GRP * N_OWN)
    counts = jnp.where(jnp.arange(N_GRP * N_OWN) == spot, MAX_TILES, counts)
    return counts.reshape(N_GRP, N_OWN).astype(jnp.int32)


def move_value(table, value, place):
    columns = jnp.arange(table.shape[1])
    present = table[:, place][:, None]
    return jnp.where(table == value, present, jnp.where(columns[None, :] == place, value, table))


def draw_matchings(key, part):
    key_rows, key_first, key_second = jax.random.split(key, 3)
    row_keys = jax.random.split(key_rows, N_GRP)
    table = jax.vmap(lambda row_key: jax.random.permutation(row_key, N_OWN - 1))(row_keys) + 1
    table = table.astype(jnp.int32)
    groups = jnp.arange(N_GRP)[:, None]
    first = jax.random.randint(key_first, (), 0, N_GRP)
    second = jax.random.randint(key_second, (), 0, N_GRP)
    table = jnp.where(groups == first, move_value(table, N_OWN - 1, 0), table)
    table = jnp.where(groups == second, move_value(table, 1, 1), table)
    return table[:, :MATCH].astype(jnp.int32)


def set_ends(drawn, key, smallest, largest):
    extent = drawn.shape
    spot = [jax.random.randint(jax.random.fold_in(key, axis), (), 0, extent[axis]) for axis in range(len(extent))]
    drawn = drawn.at[tuple(spot)].set(smallest)
    longest = extent.index(max(extent))
    spot[longest] = (spot[longest] + 1) % extent[longest]
    return drawn.at[tuple(spot)].set(largest)


def steps_of(stream_key, dims, pieces, least, top_value):
    def one(dim, blocks):
        steps = jax.random.uniform(jax.random.fold_in(jax.random.fold_in(stream_key, 6), dim), (blocks,), jnp.float32, least / len(pieces), top_value / len(pieces))
        return jnp.repeat(jnp.exp(steps), dims[dim] // blocks).reshape((-1,) + (1,) * (len(dims) - dim - 1))

    level = one(*pieces[0])
    for cut in pieces[1:]:
        level = level * one(*cut)
    return level


def scatter_about(stream_key, dims, scale, bound, cuts=(), kind=jnp.bfloat16):
    drawn = jax.random.normal(stream_key, dims, jnp.float32) * scale
    if len(cuts) > 0:
        drawn = steps_of(stream_key, dims, cuts, -0.22, 0.18) * drawn
    return jnp.clip(drawn, min=-bound, max=bound).astype(kind)


def setup_inputs(seed: int = 0) -> dict:
    splits = jax.random.split(jax.random.key(seed), 7)
    return {
        "vectors": scatter_about(splits[0], (N_OWN, K, ROWS_OWN), 1.0, 6.0, ((0, 16),), jnp.float32),
        "tiles": scatter_about(splits[1], (N_GRP, N_OWN, MAX_TILES, TILE, TILE), (N_GRP * MAX_TILES * TILE // NBLK) ** -0.5, 0.046875, ((0, 16), (1, 16)), jnp.float32),
        "tile_rows": set_ends(jax.random.randint(splits[2], (N_GRP, N_OWN, MAX_TILES), 0, NBLK), jax.random.fold_in(splits[2], 1), 0, NBLK - 1).astype(jnp.int32),
        "tile_cols": set_ends(jax.random.randint(splits[3], (N_GRP, N_OWN, MAX_TILES), 0, (MATCH + 1) * NBLK), jax.random.fold_in(splits[3], 1), 0, ((MATCH + 1) * NBLK) - 1).astype(jnp.int32),
        "tile_counts": draw_tile_counts(jax.random.fold_in(splits[6], 71), 0),
        "matchings": draw_matchings(jax.random.fold_in(splits[6], 71), 0),
    }


def device_products(tile_set, row_ids, col_ids, live_count, table, own_blocks):
    slots = jnp.arange(tile_set.shape[0], dtype=jnp.int32)
    live = slots < live_count
    x_cols = jnp.take(table, col_ids, axis=1)
    x_rows = jnp.take(own_blocks, row_ids, axis=1)
    by_rows = jnp.einsum("ktb,tab->tka", x_cols, tile_set, precision=lax.Precision.HIGHEST)
    by_cols = jnp.einsum("kta,tab->tkb", x_rows, tile_set, precision=lax.Precision.HIGHEST)
    row_hits = ((row_ids[None, :] == jnp.arange(own_blocks.shape[1], dtype=jnp.int32)[:, None]) & live[None, :]).astype(jnp.float32)
    col_hits = ((col_ids[None, :] == jnp.arange(table.shape[1], dtype=jnp.int32)[:, None]) & live[None, :]).astype(jnp.float32)
    vec_count = table.shape[0]
    self_part = jnp.einsum("rt,tka->kra", row_hits, by_rows, precision=lax.Precision.HIGHEST).reshape(vec_count, -1)
    col_parts = jnp.einsum("ct,tkb->kcb", col_hits, by_cols, precision=lax.Precision.HIGHEST)
    col_parts = col_parts.reshape(vec_count, MATCH + 1, -1)
    return self_part + col_parts[:, 0], col_parts[:, 1:]


def reference(vectors, tiles, tile_rows, tile_cols, tile_counts, matchings):
    owners = jnp.arange(N_OWN, dtype=jnp.int32)
    blocks = vectors.reshape(N_OWN, K, NBLK, TILE)

    def one_group(total, inputs):
        tile_g, rows_g, cols_g, counts_g, masks = inputs
        partners = jnp.bitwise_xor(owners[:, None], masks[None, :]).astype(jnp.int32)
        remote = blocks[partners]
        remote = jnp.transpose(remote, (0, 2, 1, 3, 4)).reshape(N_OWN, K, MATCH * NBLK, TILE)
        tables = jnp.concatenate([blocks, remote], axis=2)
        own_sum, partner_parts = jax.vmap(device_products)(tile_g, rows_g, cols_g, counts_g, tables, blocks)
        received = own_sum
        for slot in range(MATCH):
            received = received + partner_parts[partners[:, slot], :, slot]
        return total + received, None

    start = jnp.zeros((N_OWN, K, ROWS_OWN), jnp.float32)
    total, _ = lax.scan(one_group, start, (tiles, tile_rows, tile_cols, tile_counts, matchings))
    return total
```

```python
import jax
import jax.numpy as jnp
from jax import lax
from jax.experimental import pallas as pl
from jax.experimental.pallas import tpu as pltpu
from jax.sharding import Mesh, PartitionSpec as P

ZLO, X, ZHI, Y, CORE = 4, 4, 2, 4, 2
YC = Y * CORE
OWN = ZHI * YC
FAN = X * YC
GRP_AXES = ("zlo", "x")
OWN_AXES = ("zhi", "y", "core")
FAN_AXES = ("x", "y", "core")
OUT_AXES = ("zlo", "zhi", "y", "core")

REGIONS = 4
SUB = 8
LANE = 128
CHUNK = 16
GROUP = 4

VMEM = pl.BlockSpec(memory_space=pltpu.VMEM)
SMEM = pl.BlockSpec(memory_space=pltpu.SMEM)
ANY = pl.BlockSpec(memory_space=pl.ANY)

BY_COLS = (((1,), (0,)), ((), ()))
BY_ROWS = (((1,), (1,)), ((), ()))


def halves(value):
    high = value.astype(jnp.bfloat16)
    return high, (value - high.astype(jnp.float32)).astype(jnp.bfloat16)


def product(pair, high, low, dims):
    both = jnp.concatenate([high, low], axis=1 if dims is BY_COLS else 0)
    wide = lax.dot_general(pair, both, dims, preferred_element_type=jnp.float32)
    count = pair.shape[0] // 2
    return wide[:count, :LANE] + wide[count:, :LANE] + wide[:count, LANE:]


def pieces_kernel(x_ref, own_ref, out_ref):
    x = x_ref[0]
    for zlo in range(ZLO):
        start = pl.multiple_of((zlo * X + x) * LANE, LANE)
        for part in range(YC):
            block = own_ref[part * SUB : (part + 1) * SUB, pl.ds(start, LANE)]
            for zhi in range(ZHI):
                out_ref[zhi * YC + part, zlo] = block


def route_kernel(x_ref, zhi_ref, m0, m1, m2, m3, pieces_ref, out_ref):
    x = x_ref[0]
    first = zhi_ref[0] * YC
    for step, masks in enumerate((m0, m1, m2, m3)):
        base = lax.rem(x + step, X) * YC
        for slot in range(REGIONS - 1):
            mask = masks[0, slot]
            for part in range(YC):
                out_ref[base + part, slot] = pieces_ref[(first + part) ^ mask]


def collect_kernel(x_ref, zhi_ref, m0, m1, m2, m3, parts_ref, out_ref):
    x = x_ref[0]
    first = zhi_ref[0] * YC
    out_ref[...] = jnp.zeros_like(out_ref)
    for step, masks in enumerate((m0, m1, m2, m3)):
        base = lax.rem(x + step, X) * YC
        for slot in range(REGIONS):
            for part in range(YC):
                owner = first + part
                if slot > 0:
                    owner = owner ^ masks[0, slot - 1]
                for zlo in range(ZLO):
                    out_ref[zlo, owner] += parts_ref[base + part, slot, zlo]


def products_kernel(rows, cols, count, tiles, own_ref, far_ref, out_ref, held, table, sems):
    chunks = held.shape[0] // CHUNK
    copies = [
        pltpu.make_async_copy(
            tiles.at[pl.ds(i * CHUNK, CHUNK)], held.at[pl.ds(i * CHUNK, CHUNK)], sems.at[i]
        )
        for i in range(chunks)
    ]
    for copy in copies:
        copy.start()
    out_ref[...] = jnp.zeros_like(out_ref)
    vecs = own_ref.shape[0]
    blocks = own_ref.shape[1] // LANE
    for block in range(blocks):
        high, low = halves(own_ref[:, block * LANE : (block + 1) * LANE])
        table[block, :vecs] = high
        table[block, vecs:] = low
    for slot in range(REGIONS - 1):
        for block in range(blocks):
            value = jnp.concatenate(
                [far_ref[block % X * YC + part, slot, block // X] for part in range(YC)], axis=0
            )
            high, low = halves(value)
            table[(slot + 1) * blocks + block, :vecs] = high
            table[(slot + 1) * blocks + block, vecs:] = low
    live = count[0]

    def add(region, block, value):
        zlo = block // X
        base = lax.rem(block, X) * YC
        for part in range(YC):
            out_ref[base + part, region, zlo] += value[part * SUB : (part + 1) * SUB]

    def group(first, size):
        sums = []
        for k in range(size):
            row = rows[first + k]
            col = cols[first + k]
            high, low = halves(held[first + k])
            sums.append(
                (
                    row,
                    col,
                    product(table[col], high, low, BY_ROWS),
                    product(table[row], high, low, BY_COLS),
                )
            )
        for row, col, by_rows, by_cols in sums:
            add(0, row, by_rows)
            add(col // blocks, lax.rem(col, blocks), by_cols)

    for i, copy in enumerate(copies):
        copy.wait()
        here = jnp.clip(live - i * CHUNK, 0, CHUNK)
        full = here // GROUP

        def several(step, carry, i=i):
            group(i * CHUNK + step * GROUP, GROUP)
            return carry

        def single(step, carry, i=i):
            group(i * CHUNK + step, 1)
            return carry

        lax.fori_loop(0, full, several, 0)
        lax.fori_loop(full * GROUP, here, single, 0)


def exchange(value, axes):
    return lax.all_to_all(value, axes, 0, 0, tiled=False)


def on_device(vectors, tiles, tile_rows, tile_cols, tile_counts, matchings):
    own = vectors[0]
    tile_set = tiles[0, 0]
    vecs = own.shape[0]
    x = lax.axis_index("x").reshape(1).astype(jnp.int32)
    zhi = lax.axis_index("zhi").reshape(1).astype(jnp.int32)
    masks = [matchings] + [
        lax.ppermute(matchings, "x", [(i, (i - step) % X) for i in range(X)])
        for step in range(1, X)
    ]
    where = (x, zhi, *masks)
    piece = (ZLO, SUB, LANE)
    pieces = pl.pallas_call(
        pieces_kernel,
        out_shape=jax.ShapeDtypeStruct((OWN, *piece), jnp.float32),
        in_specs=[SMEM, VMEM],
        out_specs=VMEM,
        name="pieces",
    )(x, own)
    pieces = exchange(pieces, OWN_AXES)
    wanted = pl.pallas_call(
        route_kernel,
        out_shape=jax.ShapeDtypeStruct((FAN, REGIONS - 1, *piece), jnp.float32),
        in_specs=[SMEM] * 6 + [VMEM],
        out_specs=VMEM,
        name="route",
    )(*where, pieces)
    far = exchange(wanted, FAN_AXES)
    parts = pl.pallas_call(
        products_kernel,
        out_shape=jax.ShapeDtypeStruct((FAN, REGIONS, *piece), jnp.float32),
        in_specs=[SMEM] * 3 + [ANY, VMEM, VMEM],
        out_specs=VMEM,
        scratch_shapes=[
            pltpu.VMEM(tile_set.shape, jnp.float32),
            pltpu.VMEM((REGIONS * own.shape[1] // LANE, 2 * vecs, LANE), jnp.bfloat16),
            pltpu.SemaphoreType.DMA((tile_set.shape[0] // CHUNK,)),
        ],
        name="products",
    )(tile_rows[0, 0], tile_cols[0, 0], tile_counts[0], tile_set, own, far)
    parts = exchange(parts, FAN_AXES)
    sums = pl.pallas_call(
        collect_kernel,
        out_shape=jax.ShapeDtypeStruct((ZLO, OWN, SUB, LANE), jnp.float32),
        in_specs=[SMEM] * 6 + [VMEM],
        out_specs=VMEM,
        name="collect",
    )(*where, parts)
    sums = exchange(sums.reshape(ZLO * OWN, SUB, LANE), OUT_AXES)
    total = jnp.sum(sums.reshape(ZLO * ZHI, vecs, LANE), axis=0)
    return total[None]


def solution(mesh):
    fine = Mesh(mesh.devices.reshape(ZLO, X, ZHI, Y, CORE), ("zlo", "x", "zhi", "y", "core"))
    return jax.shard_map(
        on_device,
        mesh=fine,
        in_specs=(
            P(OWN_AXES, None, None),
            P(GRP_AXES, OWN_AXES, None, None, None),
            P(GRP_AXES, OWN_AXES, None),
            P(GRP_AXES, OWN_AXES, None),
            P(GRP_AXES, OWN_AXES),
            P(GRP_AXES, None),
        ),
        out_specs=P(OWN_AXES, None, GRP_AXES),
        check_vma=False,
    )
```

```python
import jax
import jax.numpy as jnp
from jax import lax
from jax.experimental import pallas as pl
from jax.experimental.pallas import tpu as pltpu
from jax.sharding import Mesh, PartitionSpec as P

ZLO, X, ZHI, Y, CORE = 4, 4, 2, 4, 2
YC = Y * CORE
OWN = ZHI * YC
FAN = X * YC
GRP_AXES = ("zlo", "x")
OWN_AXES = ("zhi", "y", "core")
FAN_AXES = ("x", "y", "core")
OUT_AXES = ("zlo", "zhi", "y", "core")

REGIONS = 4
SUB = 8
LANE = 128
CHUNK = 16
GROUP = 8
SMALL = 8 << 20
LARGE = 56 << 20

VMEM = pl.BlockSpec(memory_space=pltpu.VMEM)
SMEM = pl.BlockSpec(memory_space=pltpu.SMEM)
HBM = pl.BlockSpec(memory_space=pltpu.HBM)

BY_COLS = (((1,), (0,)), ((), ()))
BY_ROWS = (((1,), (1,)), ((), ()))


def halves(value):
    high = value.astype(jnp.bfloat16)
    return high, (value - high.astype(jnp.float32)).astype(jnp.bfloat16)


def product(pair, high, low, dims):
    both = jnp.concatenate([high, low], axis=1 if dims is BY_COLS else 0)
    wide = lax.dot_general(pair, both, dims, preferred_element_type=jnp.float32)
    count = pair.shape[0] // 2
    return wide[:count, :LANE] + wide[count:, :LANE] + wide[:count, LANE:]


def pieces_kernel(x_ref, own_ref, out_ref):
    x = x_ref[0]
    for zlo in range(ZLO):
        start = pl.multiple_of((zlo * X + x) * LANE, LANE)
        for part in range(YC):
            block = own_ref[part * SUB : (part + 1) * SUB, pl.ds(start, LANE)]
            for zhi in range(ZHI):
                out_ref[zhi * YC + part, zlo] = block


def route_kernel(x_ref, zhi_ref, m0, m1, m2, m3, pieces_ref, out_ref):
    x = x_ref[0]
    first = zhi_ref[0] * YC
    for step, masks in enumerate((m0, m1, m2, m3)):
        base = lax.rem(x + step, X) * YC
        for slot in range(REGIONS - 1):
            mask = masks[0, slot]
            for part in range(YC):
                out_ref[base + part, slot] = pieces_ref[(first + part) ^ mask]


def collect_kernel(x_ref, zhi_ref, m0, m1, m2, m3, parts_ref, out_ref):
    x = x_ref[0]
    first = zhi_ref[0] * YC
    out_ref[...] = jnp.zeros_like(out_ref)
    for step, masks in enumerate((m0, m1, m2, m3)):
        base = lax.rem(x + step, X) * YC
        for slot in range(REGIONS - 1):
            for part in range(YC):
                owner = (first + part) ^ masks[0, slot]
                for zlo in range(ZLO):
                    out_ref[zlo, owner] += parts_ref[base + part, slot, zlo]


def load_table(table, base, blocks, get, vecs):
    for block in range(blocks):
        high, low = halves(get(block))
        table[base + block, :vecs] = high
        table[base + block, vecs:] = low


def fetch(tiles, held, sems):
    copies = [
        pltpu.make_async_copy(
            tiles.at[pl.ds(i * CHUNK, CHUNK)], held.at[pl.ds(i * CHUNK, CHUNK)], sems.at[i]
        )
        for i in range(held.shape[0] // CHUNK)
    ]
    for copy in copies:
        copy.start()
    return copies


def each_group(copies, live, group):
    for i, copy in enumerate(copies):
        copy.wait()
        here = jnp.clip(live - i * CHUNK, 0, CHUNK)
        full = here // GROUP

        def several(step, carry, i=i):
            group(i * CHUNK + step * GROUP, GROUP)
            return carry

        def single(step, carry, i=i):
            group(i * CHUNK + step, 1)
            return carry

        lax.fori_loop(0, full, several, 0)
        lax.fori_loop(full * GROUP, here, single, 0)


def columns_kernel(rows, cols, count, tiles, own_ref, out_ref, self_ref, held, table, sums, sems):
    copies = fetch(tiles, held, sems)
    sums[...] = jnp.zeros_like(sums)
    vecs = own_ref.shape[0]
    blocks = own_ref.shape[1] // LANE
    load_table(table, 0, blocks, lambda b: own_ref[:, b * LANE : (b + 1) * LANE], vecs)

    def group(first, size):
        done = []
        for k in range(size):
            high, low = halves(held[first + k])
            done.append(product(table[rows[first + k]], high, low, BY_COLS))
        for k in range(size):
            col = cols[first + k]
            sums[col] += done[k]

    each_group(copies, count[0], group)
    self_ref[...] = sums[:blocks]
    for slot in range(REGIONS - 1):
        for block in range(blocks):
            zlo, x = divmod(block, X)
            value = sums[(slot + 1) * blocks + block]
            for part in range(YC):
                out_ref[x * YC + part, slot, zlo] = value[part * SUB : (part + 1) * SUB]


def rows_kernel(x_ref, rows, cols, count, tiles, own_ref, far_ref, self_ref, *rest):
    outs, (held, table, sums, sems) = rest[:X], rest[X:]
    copies = fetch(tiles, held, sems)
    sums[...] = self_ref[...]
    vecs = own_ref.shape[0]
    blocks = own_ref.shape[1] // LANE
    load_table(table, 0, blocks, lambda b: own_ref[:, b * LANE : (b + 1) * LANE], vecs)
    for slot in range(REGIONS - 1):

        def far(b, slot=slot):
            return jnp.concatenate(
                [far_ref[b % X * YC + part, slot, b // X] for part in range(YC)], axis=0
            )

        load_table(table, (slot + 1) * blocks, blocks, far, vecs)

    def group(first, size):
        done = []
        for k in range(size):
            high, low = halves(held[first + k])
            done.append(product(table[cols[first + k]], high, low, BY_ROWS))
        for k in range(size):
            row = rows[first + k]
            sums[row] += done[k]

    each_group(copies, count[0], group)
    for step in range(X):
        x = lax.rem(x_ref[0] + step, X)
        for zlo in range(ZLO):
            outs[step][zlo] = sums[zlo * X + x]


def spread_kernel(zlo_ref, a_ref, b_ref, c_ref, d_ref, *outs):
    for step in range(ZLO):
        z = zlo_ref[0] ^ step
        outs[step][...] = (a_ref[z] + b_ref[z]) + (c_ref[z] + d_ref[z])


def exchange(value, axes):
    return lax.all_to_all(value, axes, 0, 0, tiled=False)


def local(kernel, outs, specs, scratch=(), limit=None, cost=None):
    outs = [jax.ShapeDtypeStruct(shape, jnp.float32) for shape in outs]
    return pl.pallas_call(
        kernel,
        out_shape=outs,
        in_specs=specs,
        out_specs=[VMEM] * len(outs),
        scratch_shapes=scratch,
        compiler_params=pltpu.CompilerParams(vmem_limit_bytes=limit),
        cost_estimate=cost,
        name=kernel.__name__,
    )


def on_device(vectors, tiles, tile_rows, tile_cols, tile_counts, matchings):
    own = vectors[0]
    tile_set = tiles[0, 0]
    vecs, rows_own = own.shape
    slots = tile_set.shape[0]
    blocks = rows_own // LANE
    x, zhi, zlo = (
        lax.axis_index(axis).reshape(1).astype(jnp.int32) for axis in ("x", "zhi", "zlo")
    )
    masks = [matchings] + [
        lax.ppermute(matchings, "x", [(i, (i - step) % X) for i in range(X)])
        for step in range(1, X)
    ]
    where = (x, zhi, *masks)
    ids = (tile_rows[0, 0], tile_cols[0, 0], tile_counts[0])
    piece = (ZLO, SUB, LANE)
    half = pl.CostEstimate(
        flops=slots * 6 * vecs * LANE * LANE, bytes_accessed=tile_set.size * 4, transcendentals=0
    )

    def tile_scratch(operand, result):
        return [
            pltpu.VMEM(tile_set.shape, jnp.float32),
            pltpu.VMEM((operand, 2 * vecs, LANE), jnp.bfloat16),
            pltpu.VMEM((result, vecs, LANE), jnp.float32),
            pltpu.SemaphoreType.DMA((slots // CHUNK,)),
        ]

    (pieces,) = local(pieces_kernel, [(OWN, *piece)], [SMEM, VMEM], limit=SMALL)(x, own)
    pieces = exchange(pieces, OWN_AXES)
    parts, mine = local(
        columns_kernel,
        [(FAN, REGIONS - 1, *piece), (blocks, vecs, LANE)],
        [SMEM] * 3 + [HBM, VMEM],
        tile_scratch(blocks, REGIONS * blocks),
        LARGE,
        half,
    )(*ids, tile_set, own)
    parts = exchange(parts, FAN_AXES)
    (wanted,) = local(
        route_kernel, [(FAN, REGIONS - 1, *piece)], [SMEM] * 6 + [VMEM], limit=SMALL
    )(*where, pieces)
    far = exchange(wanted, FAN_AXES)
    (sums,) = local(collect_kernel, [(ZLO, OWN, SUB, LANE)], [SMEM] * 6 + [VMEM], limit=SMALL)(
        *where, parts
    )
    sums = exchange(sums.reshape(ZLO * OWN, SUB, LANE), OUT_AXES)
    rows = local(
        rows_kernel,
        [(ZLO, vecs, LANE)] * X,
        [SMEM] * 4 + [HBM, VMEM, VMEM, VMEM],
        tile_scratch(REGIONS * blocks, blocks),
        LARGE,
        half,
    )(x, *ids, tile_set, own, far, mine)
    rows = [rows[0]] + [
        lax.ppermute(rows[step], "x", [(i, (i + step) % X) for i in range(X)])
        for step in range(1, X)
    ]
    rows = local(spread_kernel, [(vecs, LANE)] * ZLO, [SMEM] + [VMEM] * X, limit=SMALL)(
        zlo, *rows
    )
    rows = [rows[0]] + [
        lax.ppermute(rows[step], "zlo", [(i, i ^ step) for i in range(ZLO)])
        for step in range(1, ZLO)
    ]
    total = jnp.sum(sums.reshape(ZLO * ZHI, vecs, LANE), axis=0)
    for row in rows:
        total = total + row
    return total[None]


def solution(mesh):
    fine = Mesh(mesh.devices.reshape(ZLO, X, ZHI, Y, CORE), ("zlo", "x", "zhi", "y", "core"))
    return jax.shard_map(
        on_device,
        mesh=fine,
        in_specs=(
            P(OWN_AXES, None, None),
            P(GRP_AXES, OWN_AXES, None, None, None),
            P(GRP_AXES, OWN_AXES, None),
            P(GRP_AXES, OWN_AXES, None),
            P(GRP_AXES, OWN_AXES),
            P(GRP_AXES, None),
        ),
        out_specs=P(OWN_AXES, None, GRP_AXES),
        check_vma=False,
    )
```

```python
import jax
import jax.numpy as jnp
from jax import lax
from jax.experimental import pallas as pl
from jax.experimental.pallas import tpu as pltpu
from jax.sharding import Mesh, PartitionSpec as P

ZLO, X, ZHI, Y, CORE = 4, 4, 2, 4, 2
YC = Y * CORE
OWN = ZHI * YC
FAN = X * YC
GRP_AXES = ("zlo", "x")
OWN_AXES = ("zhi", "y", "core")
FAN_AXES = ("x", "y", "core")
YC_AXES = ("y", "core")


REGIONS = 4
SUB = 8
LANE = 128
CHUNK = 16
GROUP = 8
SMALL = 8 << 20
LARGE = 56 << 20

VMEM = pl.BlockSpec(memory_space=pltpu.VMEM)
SMEM = pl.BlockSpec(memory_space=pltpu.SMEM)
HBM = pl.BlockSpec(memory_space=pltpu.HBM)

BY_COLS = (((1,), (0,)), ((), ()))
BY_ROWS = (((1,), (1,)), ((), ()))


def halves(value):
    high = value.astype(jnp.bfloat16)
    return high, (value - high.astype(jnp.float32)).astype(jnp.bfloat16)


def product(pair, high, low, dims):
    both = jnp.concatenate([high, low], axis=1 if dims is BY_COLS else 0)
    wide = lax.dot_general(pair, both, dims, preferred_element_type=jnp.float32)
    count = pair.shape[0] // 2
    return wide[:count, :LANE] + wide[count:, :LANE] + wide[:count, LANE:]


def pieces_kernel(x_ref, yc_ref, own_ref, *outs):
    for step in range(YC):
        row = pl.multiple_of((yc_ref[0] ^ step) * SUB, SUB)
        for zlo in range(ZLO):
            col = pl.multiple_of((zlo * X + x_ref[0]) * LANE, LANE)
            outs[step][zlo] = own_ref[pl.ds(row, SUB), pl.ds(col, LANE)]


def gather_kernel(*refs):
    for step in range(YC):
        refs[YC][step] = refs[step][...]


def route_kernel(x_ref, yc_ref, m0, m1, m2, m3, near_ref, other_ref, out_ref, held):
    held[:YC] = near_ref[...]
    held[YC:] = other_ref[...]
    for step, masks in enumerate((m0, m1, m2, m3)):
        base = lax.rem(x_ref[0] + step, X) * YC
        for slot in range(REGIONS - 1):
            mask = masks[0, slot]
            for part in range(YC):
                out_ref[base + part, slot] = held[(part ^ yc_ref[0]) ^ mask]


def collect_kernel(x_ref, yc_ref, zlo_ref, m0, m1, m2, m3, parts_ref, near_ref, other_ref, sums):
    sums[...] = jnp.zeros_like(sums)
    for step, masks in enumerate((m0, m1, m2, m3)):
        base = lax.rem(x_ref[0] + step, X) * YC
        for slot in range(REGIONS - 1):
            mask = masks[0, slot]
            for part in range(YC):
                owner = (part ^ yc_ref[0]) ^ mask
                for zlo in range(ZLO):
                    sums[zlo, owner] += parts_ref[base + part, slot, zlo]
    for step in range(ZLO):
        zlo = zlo_ref[0] ^ step
        near_ref[step] = sums[zlo, :YC]
        other_ref[step] = sums[zlo, YC:]


def add_zhi_kernel(a_ref, b_ref, *outs):
    for step in range(ZLO):
        outs[step][...] = a_ref[step] + b_ref[step]


def add_zlo_kernel(a_ref, b_ref, c_ref, d_ref, *outs):
    for step in range(YC):
        outs[step][...] = (a_ref[step] + b_ref[step]) + (c_ref[step] + d_ref[step])


def final_kernel(yc_ref, *refs):
    parts, rows, out_ref = refs[:YC], refs[YC : YC + ZLO], refs[YC + ZLO]
    for step in range(YC):
        at = pl.ds(pl.multiple_of((yc_ref[0] ^ step) * SUB, SUB), SUB)
        own = (rows[0][at] + rows[1][at]) + (rows[2][at] + rows[3][at])
        out_ref[at] = own + parts[step][...]


def load_table(table, base, blocks, get, vecs):
    for block in range(blocks):
        high, low = halves(get(block))
        table[base + block, :vecs] = high
        table[base + block, vecs:] = low


def fetch(tiles, held, sems):
    copies = [
        pltpu.make_async_copy(
            tiles.at[pl.ds(i * CHUNK, CHUNK)], held.at[pl.ds(i * CHUNK, CHUNK)], sems.at[i]
        )
        for i in range(held.shape[0] // CHUNK)
    ]
    for copy in copies:
        copy.start()
    return copies


def each_group(copies, live, group):
    for i, copy in enumerate(copies):
        copy.wait()
        here = jnp.clip(live - i * CHUNK, 0, CHUNK)
        full = here // GROUP

        def several(step, carry, i=i):
            group(i * CHUNK + step * GROUP, GROUP)
            return carry

        def single(step, carry, i=i):
            group(i * CHUNK + step, 1)
            return carry

        lax.fori_loop(0, full, several, 0)
        lax.fori_loop(full * GROUP, here, single, 0)


def columns_kernel(rows, cols, count, tiles, own_ref, out_ref, self_ref, held, table, sums, sems):
    copies = fetch(tiles, held, sems)
    sums[...] = jnp.zeros_like(sums)
    vecs = own_ref.shape[0]
    blocks = own_ref.shape[1] // LANE
    load_table(table, 0, blocks, lambda b: own_ref[:, b * LANE : (b + 1) * LANE], vecs)

    def group(first, size):
        done = []
        for k in range(size):
            high, low = halves(held[first + k])
            done.append(product(table[rows[first + k]], high, low, BY_COLS))
        for k in range(size):
            col = cols[first + k]
            sums[col] += done[k]

    each_group(copies, count[0], group)
    self_ref[...] = sums[:blocks]
    for slot in range(REGIONS - 1):
        for block in range(blocks):
            zlo, x = divmod(block, X)
            value = sums[(slot + 1) * blocks + block]
            for part in range(YC):
                out_ref[x * YC + part, slot, zlo] = value[part * SUB : (part + 1) * SUB]


def rows_kernel(x_ref, rows, cols, count, tiles, own_ref, far_ref, self_ref, *rest):
    outs, (held, table, sums, sems) = rest[:X], rest[X:]
    copies = fetch(tiles, held, sems)
    sums[...] = self_ref[...]
    vecs = own_ref.shape[0]
    blocks = own_ref.shape[1] // LANE
    load_table(table, 0, blocks, lambda b: own_ref[:, b * LANE : (b + 1) * LANE], vecs)
    for slot in range(REGIONS - 1):

        def far(b, slot=slot):
            return jnp.concatenate(
                [far_ref[b % X * YC + part, slot, b // X] for part in range(YC)], axis=0
            )

        load_table(table, (slot + 1) * blocks, blocks, far, vecs)

    def group(first, size):
        done = []
        for k in range(size):
            high, low = halves(held[first + k])
            done.append(product(table[cols[first + k]], high, low, BY_ROWS))
        for k in range(size):
            row = rows[first + k]
            sums[row] += done[k]

    each_group(copies, count[0], group)
    for step in range(X):
        x = lax.rem(x_ref[0] + step, X)
        for zlo in range(ZLO):
            outs[step][zlo] = sums[zlo * X + x]


def spread_kernel(zlo_ref, a_ref, b_ref, c_ref, d_ref, *outs):
    for step in range(ZLO):
        z = zlo_ref[0] ^ step
        outs[step][...] = (a_ref[z] + b_ref[z]) + (c_ref[z] + d_ref[z])


def exchange(value, axes):
    return lax.all_to_all(value, axes, 0, 0, tiled=False)


def local(kernel, outs, specs, scratch=(), limit=None, cost=None):
    outs = [jax.ShapeDtypeStruct(shape, jnp.float32) for shape in outs]
    return pl.pallas_call(
        kernel,
        out_shape=outs,
        in_specs=specs,
        out_specs=[VMEM] * len(outs),
        scratch_shapes=scratch,
        compiler_params=pltpu.CompilerParams(vmem_limit_bytes=limit),
        cost_estimate=cost,
    )


def swaps(arrays, axes, count):
    return [arrays[0]] + [
        lax.ppermute(arrays[step], axes, [(i, i ^ step) for i in range(count)])
        for step in range(1, count)
    ]


def on_device(vectors, tiles, tile_rows, tile_cols, tile_counts, matchings):
    own = vectors[0]
    tile_set = tiles[0, 0]
    vecs, rows_own = own.shape
    slots = tile_set.shape[0]
    blocks = rows_own // LANE
    x, zlo, yc = (
        lax.axis_index(axes).reshape(1).astype(jnp.int32) for axes in ("x", "zlo", YC_AXES)
    )
    ids = (tile_rows[0, 0], tile_cols[0, 0], tile_counts[0])
    piece = (ZLO, SUB, LANE)
    half = pl.CostEstimate(
        flops=slots * 6 * vecs * LANE * LANE, bytes_accessed=tile_set.size * 4, transcendentals=0
    )

    def tile_scratch(operand, result):
        return [
            pltpu.VMEM(tile_set.shape, jnp.float32),
            pltpu.VMEM((operand, 2 * vecs, LANE), jnp.bfloat16),
            pltpu.VMEM((result, vecs, LANE), jnp.float32),
            pltpu.SemaphoreType.DMA((slots // CHUNK,)),
        ]

    pieces = local(pieces_kernel, [piece] * YC, [SMEM] * 2 + [VMEM], limit=SMALL)(x, yc, own)
    pieces = swaps(pieces, YC_AXES, YC)
    masks = [matchings] + [
        lax.ppermute(matchings, "x", [(i, (i - step) % X) for i in range(X)])
        for step in range(1, X)
    ]
    parts, mine = local(
        columns_kernel,
        [(FAN, REGIONS - 1, *piece), (blocks, vecs, LANE)],
        [SMEM] * 3 + [HBM, VMEM],
        tile_scratch(blocks, REGIONS * blocks),
        LARGE,
        half,
    )(*ids, tile_set, own)
    (near,) = local(gather_kernel, [(YC, *piece)], [VMEM] * YC, limit=SMALL)(*pieces)
    parts, near = lax.optimization_barrier((parts, near))
    other = lax.ppermute(near, "zhi", [(0, 1), (1, 0)])
    parts = exchange(parts, FAN_AXES)
    (wanted,) = local(
        route_kernel,
        [(FAN, REGIONS - 1, *piece)],
        [SMEM] * 6 + [VMEM] * 2,
        [pltpu.VMEM((OWN, *piece), jnp.float32)],
        SMALL,
    )(x, yc, *masks, near, other)
    parts, wanted = lax.optimization_barrier((parts, wanted))
    far = exchange(wanted, FAN_AXES)
    spread = (ZLO, YC, SUB, LANE)
    near, other = local(
        collect_kernel,
        [spread] * 2,
        [SMEM] * 7 + [VMEM],
        [pltpu.VMEM((ZLO, OWN, SUB, LANE), jnp.float32)],
        SMALL,
    )(x, yc, zlo, *masks, parts)
    other = lax.ppermute(other, "zhi", [(0, 1), (1, 0)])
    parts = local(add_zhi_kernel, [spread[1:]] * ZLO, [VMEM] * 2, limit=SMALL)(near, other)
    parts = swaps(parts, "zlo", ZLO)
    parts = local(add_zlo_kernel, [spread[2:]] * YC, [VMEM] * ZLO, limit=SMALL)(*parts)
    far, *parts = lax.optimization_barrier((far, *parts))
    parts = swaps(parts, YC_AXES, YC)
    rows = local(
        rows_kernel,
        [(ZLO, vecs, LANE)] * X,
        [SMEM] * 4 + [HBM, VMEM, VMEM, VMEM],
        tile_scratch(REGIONS * blocks, blocks),
        LARGE,
        half,
    )(x, *ids, tile_set, own, far, mine)
    rows = [rows[0]] + [
        lax.ppermute(rows[step], "x", [(i, (i + step) % X) for i in range(X)])
        for step in range(1, X)
    ]
    rows = local(spread_kernel, [(vecs, LANE)] * ZLO, [SMEM] + [VMEM] * X, limit=SMALL)(
        zlo, *rows
    )
    rows = swaps(rows, "zlo", ZLO)
    (total,) = local(final_kernel, [(vecs, LANE)], [SMEM] + [VMEM] * (YC + ZLO), limit=SMALL)(
        yc, *parts, *rows
    )
    return total[None]


def solution(mesh):
    fine = Mesh(mesh.devices.reshape(ZLO, X, ZHI, Y, CORE), ("zlo", "x", "zhi", "y", "core"))
    return jax.shard_map(
        on_device,
        mesh=fine,
        in_specs=(
            P(OWN_AXES, None, None),
            P(GRP_AXES, OWN_AXES, None, None, None),
            P(GRP_AXES, OWN_AXES, None),
            P(GRP_AXES, OWN_AXES, None),
            P(GRP_AXES, OWN_AXES),
            P(GRP_AXES, None),
        ),
        out_specs=P(OWN_AXES, None, GRP_AXES),
        check_vma=False,
    )
```

```python
import jax
import jax.numpy as jnp
from jax import lax
from jax.experimental import pallas as pl
from jax.experimental.pallas import tpu as pltpu
from jax.sharding import Mesh, PartitionSpec as P

ZLO, X, ZHI, Y, CORE = 4, 4, 2, 4, 2
YC = Y * CORE
OWN = ZHI * YC
FAN = X * YC
GRP_AXES = ("zlo", "x")
OWN_AXES = ("zhi", "y", "core")
FAN_AXES = ("x", "y", "core")
OUT_AXES = ("zlo", "zhi", "y", "core")

REGIONS = 4
SUB = 8
LANE = 128
CHUNK = 16
GROUP = 8
SMALL = 8 << 20
LARGE = 56 << 20

VMEM = pl.BlockSpec(memory_space=pltpu.VMEM)
SMEM = pl.BlockSpec(memory_space=pltpu.SMEM)
HBM = pl.BlockSpec(memory_space=pltpu.HBM)

BY_COLS = (((1,), (0,)), ((), ()))
BY_ROWS = (((1,), (1,)), ((), ()))


def halves(value):
    high = value.astype(jnp.bfloat16)
    return high, (value - high.astype(jnp.float32)).astype(jnp.bfloat16)


def product(pair, high, low, dims):
    both = jnp.concatenate([high, low], axis=1 if dims is BY_COLS else 0)
    wide = lax.dot_general(pair, both, dims, preferred_element_type=jnp.float32)
    count = pair.shape[0] // 2
    return wide[:count, :LANE] + wide[count:, :LANE] + wide[:count, LANE:]


def pieces_kernel(x_ref, own_ref, out_ref):
    x = x_ref[0]
    for zlo in range(ZLO):
        start = pl.multiple_of((zlo * X + x) * LANE, LANE)
        for part in range(YC):
            block = own_ref[part * SUB : (part + 1) * SUB, pl.ds(start, LANE)]
            for zhi in range(ZHI):
                out_ref[zhi * YC + part, zlo] = block


def route_kernel(x_ref, zhi_ref, m0, m1, m2, m3, pieces_ref, out_ref):
    x = x_ref[0]
    first = zhi_ref[0] * YC
    for step, masks in enumerate((m0, m1, m2, m3)):
        base = lax.rem(x + step, X) * YC
        for slot in range(REGIONS - 1):
            mask = masks[0, slot]
            for part in range(YC):
                out_ref[base + part, slot] = pieces_ref[(first + part) ^ mask]


def collect_kernel(x_ref, zhi_ref, m0, m1, m2, m3, parts_ref, out_ref):
    x = x_ref[0]
    first = zhi_ref[0] * YC
    out_ref[...] = jnp.zeros_like(out_ref)
    for step, masks in enumerate((m0, m1, m2, m3)):
        base = lax.rem(x + step, X) * YC
        for slot in range(REGIONS - 1):
            for part in range(YC):
                owner = (first + part) ^ masks[0, slot]
                for zlo in range(ZLO):
                    out_ref[zlo, owner] += parts_ref[base + part, slot, zlo]


def load_table(table, base, blocks, get, vecs):
    for block in range(blocks):
        high, low = halves(get(block))
        table[base + block, :vecs] = high
        table[base + block, vecs:] = low


def fetch(tiles, held, sems):
    copies = [
        pltpu.make_async_copy(
            tiles.at[pl.ds(i * CHUNK, CHUNK)], held.at[pl.ds(i * CHUNK, CHUNK)], sems.at[i]
        )
        for i in range(held.shape[0] // CHUNK)
    ]
    for copy in copies:
        copy.start()
    return copies


def each_group(copies, live, group):
    for i, copy in enumerate(copies):
        copy.wait()
        here = jnp.clip(live - i * CHUNK, 0, CHUNK)
        full = here // GROUP

        def several(step, carry, i=i):
            group(i * CHUNK + step * GROUP, GROUP)
            return carry

        def single(step, carry, i=i):
            group(i * CHUNK + step, 1)
            return carry

        lax.fori_loop(0, full, several, 0)
        lax.fori_loop(full * GROUP, here, single, 0)


def columns_kernel(rows, cols, count, tiles, own_ref, out_ref, self_ref, held, table, sums, sems):
    copies = fetch(tiles, held, sems)
    sums[...] = jnp.zeros_like(sums)
    vecs = own_ref.shape[0]
    blocks = own_ref.shape[1] // LANE
    load_table(table, 0, blocks, lambda b: own_ref[:, b * LANE : (b + 1) * LANE], vecs)

    def group(first, size):
        done = []
        for k in range(size):
            high, low = halves(held[first + k])
            done.append(product(table[rows[first + k]], high, low, BY_COLS))
        for k in range(size):
            col = cols[first + k]
            sums[col] += done[k]

    each_group(copies, count[0], group)
    self_ref[...] = sums[:blocks]
    for slot in range(REGIONS - 1):
        for block in range(blocks):
            zlo, x = divmod(block, X)
            value = sums[(slot + 1) * blocks + block]
            for part in range(YC):
                out_ref[x * YC + part, slot, zlo] = value[part * SUB : (part + 1) * SUB]


def rows_kernel(zlo_ref, rows, cols, count, tiles, own_ref, far_ref, self_ref, *rest):
    outs, (held, table, sums, sems) = rest[:ZLO], rest[ZLO:]
    copies = fetch(tiles, held, sems)
    sums[...] = self_ref[...]
    vecs = own_ref.shape[0]
    blocks = own_ref.shape[1] // LANE
    load_table(table, 0, blocks, lambda b: own_ref[:, b * LANE : (b + 1) * LANE], vecs)
    for slot in range(REGIONS - 1):

        def far(b, slot=slot):
            return jnp.concatenate(
                [far_ref[b % X * YC + part, slot, b // X] for part in range(YC)], axis=0
            )

        load_table(table, (slot + 1) * blocks, blocks, far, vecs)

    def group(first, size):
        done = []
        for k in range(size):
            high, low = halves(held[first + k])
            done.append(product(table[cols[first + k]], high, low, BY_ROWS))
        for k in range(size):
            row = rows[first + k]
            sums[row] += done[k]

    each_group(copies, count[0], group)
    for step in range(ZLO):
        first = (zlo_ref[0] ^ step) * X
        for x in range(X):
            outs[step][x] = sums[first + x]


def spread_kernel(x_ref, a_ref, b_ref, c_ref, d_ref, *outs):
    for step in range(X):
        x = x_ref[0] ^ step
        outs[step][...] = (a_ref[x] + b_ref[x]) + (c_ref[x] + d_ref[x])


def swaps(arrays, axis, count):
    return [arrays[0]] + [
        lax.ppermute(arrays[step], axis, [(i, i ^ step) for i in range(count)])
        for step in range(1, count)
    ]


def exchange(value, axes):
    return lax.all_to_all(value, axes, 0, 0, tiled=False)


def local(kernel, outs, specs, scratch=(), limit=None, cost=None):
    outs = [jax.ShapeDtypeStruct(shape, jnp.float32) for shape in outs]
    return pl.pallas_call(
        kernel,
        out_shape=outs,
        in_specs=specs,
        out_specs=[VMEM] * len(outs),
        scratch_shapes=scratch,
        compiler_params=pltpu.CompilerParams(vmem_limit_bytes=limit),
        cost_estimate=cost,
        name=kernel.__name__,
    )


def on_device(vectors, tiles, tile_rows, tile_cols, tile_counts, matchings):
    own = vectors[0]
    tile_set = tiles[0, 0]
    vecs, rows_own = own.shape
    slots = tile_set.shape[0]
    blocks = rows_own // LANE
    x, zhi, zlo = (
        lax.axis_index(axis).reshape(1).astype(jnp.int32) for axis in ("x", "zhi", "zlo")
    )
    masks = [matchings] + [
        lax.ppermute(matchings, "x", [(i, (i - step) % X) for i in range(X)])
        for step in range(1, X)
    ]
    where = (x, zhi, *masks)
    ids = (tile_rows[0, 0], tile_cols[0, 0], tile_counts[0])
    piece = (ZLO, SUB, LANE)
    half = pl.CostEstimate(
        flops=slots * 6 * vecs * LANE * LANE, bytes_accessed=tile_set.size * 4, transcendentals=0
    )

    def tile_scratch(operand, result):
        return [
            pltpu.VMEM(tile_set.shape, jnp.float32),
            pltpu.VMEM((operand, 2 * vecs, LANE), jnp.bfloat16),
            pltpu.VMEM((result, vecs, LANE), jnp.float32),
            pltpu.SemaphoreType.DMA((slots // CHUNK,)),
        ]

    (pieces,) = local(pieces_kernel, [(OWN, *piece)], [SMEM, VMEM], limit=SMALL)(x, own)
    pieces = exchange(pieces, OWN_AXES)
    parts, mine = local(
        columns_kernel,
        [(FAN, REGIONS - 1, *piece), (blocks, vecs, LANE)],
        [SMEM] * 3 + [HBM, VMEM],
        tile_scratch(blocks, REGIONS * blocks),
        LARGE,
        half,
    )(*ids, tile_set, own)
    (wanted,) = local(
        route_kernel, [(FAN, REGIONS - 1, *piece)], [SMEM] * 6 + [VMEM], limit=SMALL
    )(*where, pieces)
    far = exchange(wanted, FAN_AXES)
    far, parts = lax.optimization_barrier((far, parts))
    parts = exchange(parts, FAN_AXES)
    rows = local(
        rows_kernel,
        [(X, vecs, LANE)] * ZLO,
        [SMEM] * 4 + [HBM, VMEM, VMEM, VMEM],
        tile_scratch(REGIONS * blocks, blocks),
        LARGE,
        half,
    )(zlo, *ids, tile_set, own, far, mine)
    rows = swaps(rows, "zlo", ZLO)
    rows = local(spread_kernel, [(vecs, LANE)] * X, [SMEM] + [VMEM] * ZLO, limit=SMALL)(x, *rows)
    parts, *rows = lax.optimization_barrier((parts, *rows))
    (sums,) = local(collect_kernel, [(ZLO, OWN, SUB, LANE)], [SMEM] * 6 + [VMEM], limit=SMALL)(
        *where, parts
    )
    sums = exchange(sums.reshape(ZLO * OWN, SUB, LANE), OUT_AXES)
    rows = swaps(rows, "x", X)
    total = jnp.sum(sums.reshape(ZLO * ZHI, vecs, LANE), axis=0)
    for row in rows:
        total = total + row
    return total[None]


def solution(mesh):
    fine = Mesh(mesh.devices.reshape(ZLO, X, ZHI, Y, CORE), ("zlo", "x", "zhi", "y", "core"))
    return jax.shard_map(
        on_device,
        mesh=fine,
        in_specs=(
            P(OWN_AXES, None, None),
            P(GRP_AXES, OWN_AXES, None, None, None),
            P(GRP_AXES, OWN_AXES, None),
            P(GRP_AXES, OWN_AXES, None),
            P(GRP_AXES, OWN_AXES),
            P(GRP_AXES, None),
        ),
        out_specs=P(OWN_AXES, None, GRP_AXES),
        check_vma=False,
    )
```

```python
import jax
import jax.numpy as jnp
from jax import lax
from jax.experimental import pallas as pl
from jax.experimental.pallas import tpu as pltpu
from jax.sharding import Mesh, PartitionSpec as P

ZLO, X, ZHI, Y, CORE = 4, 4, 2, 4, 2
YC = Y * CORE
OWN = ZHI * YC
FAN = X * YC
GRP_AXES = ("zlo", "x")
OWN_AXES = ("zhi", "y", "core")
FAN_AXES = ("x", "y", "core")
YC_AXES = ("y", "core")


REGIONS = 4
SUB = 8
LANE = 128
CHUNK = 16
GROUP = 8
SMALL = 8 << 20
LARGE = 56 << 20
FULL = 60 << 20
ROWS = 52 << 20

VMEM = pl.BlockSpec(memory_space=pltpu.VMEM)
SMEM = pl.BlockSpec(memory_space=pltpu.SMEM)
HBM = pl.BlockSpec(memory_space=pltpu.HBM)

BY_COLS = (((1,), (0,)), ((), ()))
BY_ROWS = (((1,), (1,)), ((), ()))


def halves(value):
    high = value.astype(jnp.bfloat16)
    return high, (value - high.astype(jnp.float32)).astype(jnp.bfloat16)


def product(pair, high, low, dims):
    both = jnp.concatenate([high, low], axis=1 if dims is BY_COLS else 0)
    wide = lax.dot_general(pair, both, dims, preferred_element_type=jnp.float32)
    count = pair.shape[0] // 2
    return wide[:count, :LANE] + wide[count:, :LANE] + wide[:count, LANE:]


def pieces_kernel(x_ref, yc_ref, own_ref, out_ref, held, sems):
    copies = []
    for zlo in range(ZLO):
        col = pl.multiple_of((zlo * X + x_ref[0]) * LANE, LANE)
        copies.append(
            pltpu.make_async_copy(own_ref.at[:, pl.ds(col, LANE)], held.at[zlo], sems.at[zlo])
        )
    for copy in copies:
        copy.start()
    for copy in copies:
        copy.wait()
    for step in range(YC):
        row = pl.multiple_of((yc_ref[0] ^ step) * SUB, SUB)
        for zlo in range(ZLO):
            out_ref[step, zlo] = held[zlo, pl.ds(row, SUB)]


def pair_kernel(near_ref, other_ref, *outs):
    for step in range(YC):
        outs[step][0] = near_ref[step]
        outs[step][1] = other_ref[step]


def route_kernel(x_ref, yc_ref, m0, m1, m2, m3, *refs):
    pieces, out_ref, held = refs[:YC], refs[YC], refs[YC + 1]
    for step in range(YC):
        for zhi in range(ZHI):
            held[zhi * YC + step] = pieces[step][zhi]
    for step, masks in enumerate((m0, m1, m2, m3)):
        base = lax.rem(x_ref[0] + step, X) * YC
        for slot in range(REGIONS - 1):
            mask = masks[0, slot]
            for part in range(YC):
                out_ref[base + part, slot] = held[(part ^ yc_ref[0]) ^ mask]


def collect_kernel(x_ref, yc_ref, zlo_ref, m0, m1, m2, m3, parts_ref, near_ref, other_ref, sums):
    sums[...] = jnp.zeros_like(sums)
    for step, masks in enumerate((m0, m1, m2, m3)):
        base = lax.rem(x_ref[0] + step, X) * YC
        for slot in range(REGIONS - 1):
            mask = masks[0, slot]
            for part in range(YC):
                owner = (part ^ yc_ref[0]) ^ mask
                for zlo in range(ZLO):
                    sums[zlo, owner] += parts_ref[base + part, slot, zlo]
    for step in range(ZLO):
        zlo = zlo_ref[0] ^ step
        near_ref[step] = sums[zlo, :YC]
        other_ref[step] = sums[zlo, YC:]


def add_zhi_kernel(a_ref, b_ref, *outs):
    for step in range(ZLO):
        outs[step][...] = a_ref[step] + b_ref[step]


def add_zlo_kernel(a_ref, b_ref, c_ref, d_ref, *outs):
    for step in range(YC):
        outs[step][...] = (a_ref[step] + b_ref[step]) + (c_ref[step] + d_ref[step])


def final_kernel(yc_ref, rows_ref, *refs):
    parts, out_ref = refs[:YC], refs[YC]
    for step in range(YC):
        at = pl.ds(pl.multiple_of((yc_ref[0] ^ step) * SUB, SUB), SUB)
        total = parts[step][...]
        for group in range(rows_ref.shape[0]):
            total = total + rows_ref[group, at]
        out_ref[at] = total


def load_table(table, base, blocks, get, vecs):
    for block in range(blocks):
        high, low = halves(get(block))
        table[base + block, :vecs] = high
        table[base + block, vecs:] = low


def fetch(tiles, held, sems):
    copies = [
        pltpu.make_async_copy(
            tiles.at[pl.ds(i * CHUNK, CHUNK)], held.at[pl.ds(i * CHUNK, CHUNK)], sems.at[i]
        )
        for i in range(held.shape[0] // CHUNK)
    ]
    for copy in copies:
        copy.start()
    return copies


def each_group(copies, live, group):
    for i, copy in enumerate(copies):
        copy.wait()
        here = jnp.clip(live - i * CHUNK, 0, CHUNK)
        full = here // GROUP

        def several(step, carry, i=i):
            group(i * CHUNK + step * GROUP, GROUP)
            return carry

        def single(step, carry, i=i):
            group(i * CHUNK + step, 1)
            return carry

        lax.fori_loop(0, full, several, 0)
        lax.fori_loop(full * GROUP, here, single, 0)


def columns_kernel(rows, cols, count, tiles, own_ref, out_ref, self_ref, held, table, sums, sems):
    copies = fetch(tiles, held, sems)
    sums[...] = jnp.zeros_like(sums)
    vecs = own_ref.shape[0]
    blocks = own_ref.shape[1] // LANE
    load_table(table, 0, blocks, lambda b: own_ref[:, b * LANE : (b + 1) * LANE], vecs)

    def group(first, size):
        done = []
        for k in range(size):
            high, low = halves(held[first + k])
            done.append(product(table[rows[first + k]], high, low, BY_COLS))
        for k in range(size):
            col = cols[first + k]
            sums[col] += done[k]

    each_group(copies, count[0], group)
    self_ref[...] = sums[:blocks]
    for slot in range(REGIONS - 1):
        for block in range(blocks):
            zlo, x = divmod(block, X)
            value = sums[(slot + 1) * blocks + block]
            for part in range(YC):
                out_ref[x * YC + part, slot, zlo] = value[part * SUB : (part + 1) * SUB]


def rows_kernel(rows, cols, count, tiles, own_ref, far_ref, self_ref, sums, held, table, sems):
    copies = fetch(tiles, held, sems)
    sums[...] = self_ref[...]
    vecs = own_ref.shape[0]
    blocks = own_ref.shape[1] // LANE
    load_table(table, 0, blocks, lambda b: own_ref[:, b * LANE : (b + 1) * LANE], vecs)
    for slot in range(REGIONS - 1):

        def far(b, slot=slot):
            return jnp.concatenate(
                [far_ref[b % X * YC + part, slot, b // X] for part in range(YC)], axis=0
            )

        load_table(table, (slot + 1) * blocks, blocks, far, vecs)

    def group(first, size):
        done = []
        for k in range(size):
            high, low = halves(held[first + k])
            done.append(product(table[cols[first + k]], high, low, BY_ROWS))
        for k in range(size):
            row = rows[first + k]
            sums[row] += done[k]

    each_group(copies, count[0], group)


def exchange(value, axes):
    return lax.all_to_all(value, axes, 0, 0, tiled=False)


def local(kernel, outs, specs, scratch=(), limit=None, cost=None):
    outs = [jax.ShapeDtypeStruct(shape, jnp.float32) for shape in outs]
    return pl.pallas_call(
        kernel,
        out_shape=outs,
        in_specs=specs,
        out_specs=[VMEM] * len(outs),
        scratch_shapes=scratch,
        compiler_params=pltpu.CompilerParams(vmem_limit_bytes=limit),
        cost_estimate=cost,
        name=kernel.__name__,
    )


def swaps(arrays, axes, count):
    return [arrays[0]] + [
        lax.ppermute(arrays[step], axes, [(i, i ^ step) for i in range(count)])
        for step in range(1, count)
    ]


def on_device(vectors, tiles, tile_rows, tile_cols, tile_counts, matchings):
    own = vectors[0]
    tile_set = tiles[0, 0]
    vecs, rows_own = own.shape
    slots = tile_set.shape[0]
    blocks = rows_own // LANE
    x, zlo, yc = (
        lax.axis_index(axes).reshape(1).astype(jnp.int32) for axes in ("x", "zlo", YC_AXES)
    )
    ids = (tile_rows[0, 0], tile_cols[0, 0], tile_counts[0])
    piece = (ZLO, SUB, LANE)
    half = pl.CostEstimate(
        flops=slots * 6 * vecs * LANE * LANE, bytes_accessed=tile_set.size * 4, transcendentals=0
    )

    def tile_scratch(operand, result):
        sums = [pltpu.VMEM((result, vecs, LANE), jnp.float32)] if result else []
        return [
            pltpu.VMEM(tile_set.shape, jnp.float32),
            pltpu.VMEM((operand, 2 * vecs, LANE), jnp.bfloat16),
            *sums,
            pltpu.SemaphoreType.DMA((slots // CHUNK,)),
        ]

    whole = (YC, *piece)
    (near,) = local(
        pieces_kernel,
        [whole],
        [SMEM] * 2 + [HBM],
        [pltpu.VMEM((ZLO, vecs, LANE), jnp.float32), pltpu.SemaphoreType.DMA((ZLO,))],
        FULL,
    )(x, yc, own)
    other = lax.ppermute(near, "zhi", [(0, 1), (1, 0)])
    masks = [matchings] + [
        lax.ppermute(matchings, "x", [(i, (i - step) % X) for i in range(X)])
        for step in range(1, X)
    ]
    parts, mine = local(
        columns_kernel,
        [(FAN, REGIONS - 1, *piece), (blocks, vecs, LANE)],
        [SMEM] * 3 + [HBM, VMEM],
        tile_scratch(blocks, REGIONS * blocks),
        LARGE,
        half,
    )(*ids, tile_set, own)
    parts = exchange(parts, FAN_AXES)
    pieces = local(pair_kernel, [(ZHI, *piece)] * YC, [VMEM] * 2, limit=SMALL)(near, other)
    pieces = swaps(pieces, YC_AXES, YC)
    (wanted,) = local(
        route_kernel,
        [(FAN, REGIONS - 1, *piece)],
        [SMEM] * 6 + [VMEM] * YC,
        [pltpu.VMEM((OWN, *piece), jnp.float32)],
        SMALL,
    )(x, yc, *masks, *pieces)
    parts, wanted = lax.optimization_barrier((parts, wanted))
    far = exchange(wanted, FAN_AXES)
    spread = (ZLO, YC, SUB, LANE)
    near, other = local(
        collect_kernel,
        [spread] * 2,
        [SMEM] * 7 + [VMEM],
        [pltpu.VMEM((ZLO, OWN, SUB, LANE), jnp.float32)],
        SMALL,
    )(x, yc, zlo, *masks, parts)
    other = lax.ppermute(other, "zhi", [(0, 1), (1, 0)])
    parts = local(add_zhi_kernel, [spread[1:]] * ZLO, [VMEM] * 2, limit=SMALL)(near, other)
    parts = swaps(parts, "zlo", ZLO)
    parts = local(add_zlo_kernel, [spread[2:]] * YC, [VMEM] * ZLO, limit=SMALL)(*parts)
    far, *parts = lax.optimization_barrier((far, *parts))
    (rows,) = local(
        rows_kernel,
        [(blocks, vecs, LANE)],
        [SMEM] * 3 + [HBM, VMEM, VMEM, VMEM],
        tile_scratch(REGIONS * blocks, None),
        ROWS,
        half,
    )(*ids, tile_set, own, far, mine)
    rows, *parts = lax.optimization_barrier((rows, *parts))
    rows = exchange(rows, GRP_AXES)
    parts = swaps(parts, YC_AXES, YC)
    (total,) = local(final_kernel, [(vecs, LANE)], [SMEM] + [VMEM] * (1 + YC), limit=SMALL)(
        yc, rows, *parts
    )
    return total[None]


def solution(mesh):
    fine = Mesh(mesh.devices.reshape(ZLO, X, ZHI, Y, CORE), ("zlo", "x", "zhi", "y", "core"))
    return jax.shard_map(
        on_device,
        mesh=fine,
        in_specs=(
            P(OWN_AXES, None, None),
            P(GRP_AXES, OWN_AXES, None, None, None),
            P(GRP_AXES, OWN_AXES, None),
            P(GRP_AXES, OWN_AXES, None),
            P(GRP_AXES, OWN_AXES),
            P(GRP_AXES, None),
        ),
        out_specs=P(OWN_AXES, None, GRP_AXES),
        check_vma=False,
    )
```

```python
import jax
import jax.numpy as jnp
from jax import lax
from jax.experimental import pallas as pl
from jax.experimental.pallas import tpu as pltpu
from jax.sharding import Mesh, PartitionSpec as P

ZLO, X, ZHI, Y, CORE = 4, 4, 2, 4, 2
YC = Y * CORE
OWN = ZHI * YC
FAN = X * YC
GRP_AXES = ("zlo", "x")
OWN_AXES = ("zhi", "y", "core")
FAN_AXES = ("x", "y", "core")
YC_AXES = ("y", "core")


REGIONS = 4
SUB = 8
LANE = 128
CHUNK = 16
GROUP = 8
SMALL = 8 << 20
LARGE = 56 << 20
ROWS = 52 << 20

VMEM = pl.BlockSpec(memory_space=pltpu.VMEM)
SMEM = pl.BlockSpec(memory_space=pltpu.SMEM)
HBM = pl.BlockSpec(memory_space=pltpu.HBM)

BY_COLS = (((1,), (0,)), ((), ()))
BY_ROWS = (((1,), (1,)), ((), ()))


def halves(value):
    high = value.astype(jnp.bfloat16)
    return high, (value - high.astype(jnp.float32)).astype(jnp.bfloat16)


def product(pair, high, low, dims):
    both = jnp.concatenate([high, low], axis=1 if dims is BY_COLS else 0)
    wide = lax.dot_general(pair, both, dims, preferred_element_type=jnp.float32)
    count = pair.shape[0] // 2
    return wide[:count, :LANE] + wide[count:, :LANE] + wide[:count, LANE:]


def pieces_kernel(x_ref, yc_ref, own_ref, out_ref, held, sems):
    copies = []
    for zlo in range(ZLO):
        col = pl.multiple_of((zlo * X + x_ref[0]) * LANE, LANE)
        copies.append(
            pltpu.make_async_copy(own_ref.at[:, pl.ds(col, LANE)], held.at[zlo], sems.at[zlo])
        )
    for copy in copies:
        copy.start()
    for copy in copies:
        copy.wait()
    for step in range(YC):
        row = pl.multiple_of((yc_ref[0] ^ step) * SUB, SUB)
        for zlo in range(ZLO):
            out_ref[step, zlo] = held[zlo, pl.ds(row, SUB)]


def pair_kernel(near_ref, other_ref, *outs):
    for step in range(YC):
        outs[step][0] = near_ref[step]
        outs[step][1] = other_ref[step]


def route_kernel(x_ref, yc_ref, m0, m1, m2, m3, *refs):
    pieces, out_ref, held = refs[:YC], refs[YC], refs[YC + 1]
    for step in range(YC):
        for zhi in range(ZHI):
            held[zhi * YC + step] = pieces[step][zhi]
    for step, masks in enumerate((m0, m1, m2, m3)):
        base = lax.rem(x_ref[0] + step, X) * YC
        for slot in range(REGIONS - 1):
            mask = masks[0, slot]
            for part in range(YC):
                out_ref[base + part, slot] = held[(part ^ yc_ref[0]) ^ mask]


def collect_kernel(x_ref, yc_ref, zlo_ref, m0, m1, m2, m3, parts_ref, near_ref, other_ref, sums):
    sums[...] = jnp.zeros_like(sums)
    for step, masks in enumerate((m0, m1, m2, m3)):
        base = lax.rem(x_ref[0] + step, X) * YC
        for slot in range(REGIONS - 1):
            mask = masks[0, slot]
            for part in range(YC):
                owner = (part ^ yc_ref[0]) ^ mask
                for zlo in range(ZLO):
                    sums[zlo, owner] += parts_ref[base + part, slot, zlo]
    for step in range(ZLO):
        zlo = zlo_ref[0] ^ step
        near_ref[step] = sums[zlo, :YC]
        other_ref[step] = sums[zlo, YC:]


def add_zhi_kernel(a_ref, b_ref, *outs):
    for step in range(ZLO):
        outs[step][...] = a_ref[step] + b_ref[step]


def add_zlo_kernel(a_ref, b_ref, c_ref, d_ref, *outs):
    for step in range(YC):
        outs[step][...] = (a_ref[step] + b_ref[step]) + (c_ref[step] + d_ref[step])


def final_kernel(yc_ref, rows_ref, *refs):
    parts, out_ref = refs[:YC], refs[YC]
    for step in range(YC):
        at = pl.ds(pl.multiple_of((yc_ref[0] ^ step) * SUB, SUB), SUB)
        total = parts[step][...]
        for group in range(rows_ref.shape[0]):
            total = total + rows_ref[group, at]
        out_ref[at] = total


def load_table(table, base, blocks, get, vecs):
    for block in range(blocks):
        high, low = halves(get(block))
        table[base + block, :vecs] = high
        table[base + block, vecs:] = low


def fetch(tiles, held, sems):
    copies = [
        pltpu.make_async_copy(
            tiles.at[pl.ds(i * CHUNK, CHUNK)], held.at[pl.ds(i * CHUNK, CHUNK)], sems.at[i]
        )
        for i in range(held.shape[0] // CHUNK)
    ]
    for copy in copies:
        copy.start()
    return copies


def each_group(copies, live, group):
    for i, copy in enumerate(copies):
        copy.wait()
        here = jnp.clip(live - i * CHUNK, 0, CHUNK)
        full = here // GROUP

        def several(step, carry, i=i):
            group(i * CHUNK + step * GROUP, GROUP)
            return carry

        def single(step, carry, i=i):
            group(i * CHUNK + step, 1)
            return carry

        lax.fori_loop(0, full, several, 0)
        lax.fori_loop(full * GROUP, here, single, 0)


def columns_kernel(rows, cols, count, tiles, own_ref, out_ref, self_ref, held, table, sums, sems):
    copies = fetch(tiles, held, sems)
    sums[...] = jnp.zeros_like(sums)
    vecs = own_ref.shape[0]
    blocks = own_ref.shape[1] // LANE
    load_table(table, 0, blocks, lambda b: own_ref[:, b * LANE : (b + 1) * LANE], vecs)

    def group(first, size):
        done = []
        for k in range(size):
            high, low = halves(held[first + k])
            done.append(product(table[rows[first + k]], high, low, BY_COLS))
        for k in range(size):
            col = cols[first + k]
            sums[col] += done[k]

    each_group(copies, count[0], group)
    self_ref[...] = sums[:blocks]
    for slot in range(REGIONS - 1):
        for block in range(blocks):
            zlo, x = divmod(block, X)
            value = sums[(slot + 1) * blocks + block]
            for part in range(YC):
                out_ref[x * YC + part, slot, zlo] = value[part * SUB : (part + 1) * SUB]


def rows_kernel(rows, cols, count, tiles, own_ref, far_ref, self_ref, sums, held, table, sems):
    copies = fetch(tiles, held, sems)
    sums[...] = self_ref[...]
    vecs = own_ref.shape[0]
    blocks = own_ref.shape[1] // LANE
    load_table(table, 0, blocks, lambda b: own_ref[:, b * LANE : (b + 1) * LANE], vecs)
    for slot in range(REGIONS - 1):

        def far(b, slot=slot):
            return jnp.concatenate(
                [far_ref[b % X * YC + part, slot, b // X] for part in range(YC)], axis=0
            )

        load_table(table, (slot + 1) * blocks, blocks, far, vecs)

    def group(first, size):
        done = []
        for k in range(size):
            high, low = halves(held[first + k])
            done.append(product(table[cols[first + k]], high, low, BY_ROWS))
        for k in range(size):
            row = rows[first + k]
            sums[row] += done[k]

    each_group(copies, count[0], group)


def exchange(value, axes):
    return lax.all_to_all(value, axes, 0, 0, tiled=False)


def local(kernel, outs, specs, scratch=(), limit=None, cost=None):
    outs = [jax.ShapeDtypeStruct(shape, jnp.float32) for shape in outs]
    return pl.pallas_call(
        kernel,
        out_shape=outs,
        in_specs=specs,
        out_specs=[VMEM] * len(outs),
        scratch_shapes=scratch,
        compiler_params=pltpu.CompilerParams(vmem_limit_bytes=limit),
        cost_estimate=cost,
    )


def swaps(arrays, axes, count):
    return [arrays[0]] + [
        lax.ppermute(arrays[step], axes, [(i, i ^ step) for i in range(count)])
        for step in range(1, count)
    ]


def on_device(vectors, tiles, tile_rows, tile_cols, tile_counts, matchings):
    own = vectors[0]
    tile_set = tiles[0, 0]
    vecs, rows_own = own.shape
    slots = tile_set.shape[0]
    blocks = rows_own // LANE
    x, zlo, yc = (
        lax.axis_index(axes).reshape(1).astype(jnp.int32) for axes in ("x", "zlo", YC_AXES)
    )
    ids = (tile_rows[0, 0], tile_cols[0, 0], tile_counts[0])
    piece = (ZLO, SUB, LANE)
    half = pl.CostEstimate(
        flops=slots * 6 * vecs * LANE * LANE, bytes_accessed=tile_set.size * 4, transcendentals=0
    )

    def tile_scratch(operand, result):
        sums = [pltpu.VMEM((result, vecs, LANE), jnp.float32)] if result else []
        return [
            pltpu.VMEM(tile_set.shape, jnp.float32),
            pltpu.VMEM((operand, 2 * vecs, LANE), jnp.bfloat16),
            *sums,
            pltpu.SemaphoreType.DMA((slots // CHUNK,)),
        ]

    whole = (YC, *piece)
    (near,) = local(
        pieces_kernel,
        [whole],
        [SMEM] * 2 + [HBM],
        [pltpu.VMEM((ZLO, vecs, LANE), jnp.float32), pltpu.SemaphoreType.DMA((ZLO,))],
        SMALL,
    )(x, yc, own)
    other = lax.ppermute(near, "zhi", [(0, 1), (1, 0)])
    masks = [matchings] + [
        lax.ppermute(matchings, "x", [(i, (i - step) % X) for i in range(X)])
        for step in range(1, X)
    ]
    parts, mine = local(
        columns_kernel,
        [(FAN, REGIONS - 1, *piece), (blocks, vecs, LANE)],
        [SMEM] * 3 + [HBM, VMEM],
        tile_scratch(blocks, REGIONS * blocks),
        LARGE,
        half,
    )(*ids, tile_set, own)
    parts = exchange(parts, FAN_AXES)
    pieces = local(pair_kernel, [(ZHI, *piece)] * YC, [VMEM] * 2, limit=SMALL)(near, other)
    pieces = swaps(pieces, YC_AXES, YC)
    (wanted,) = local(
        route_kernel,
        [(FAN, REGIONS - 1, *piece)],
        [SMEM] * 6 + [VMEM] * YC,
        [pltpu.VMEM((OWN, *piece), jnp.float32)],
        SMALL,
    )(x, yc, *masks, *pieces)
    parts, wanted = lax.optimization_barrier((parts, wanted))
    far = exchange(wanted, FAN_AXES)
    spread = (ZLO, YC, SUB, LANE)
    near, other = local(
        collect_kernel,
        [spread] * 2,
        [SMEM] * 7 + [VMEM],
        [pltpu.VMEM((ZLO, OWN, SUB, LANE), jnp.float32)],
        SMALL,
    )(x, yc, zlo, *masks, parts)
    other = lax.ppermute(other, "zhi", [(0, 1), (1, 0)])
    parts = local(add_zhi_kernel, [spread[1:]] * ZLO, [VMEM] * 2, limit=SMALL)(near, other)
    parts = swaps(parts, "zlo", ZLO)
    parts = local(add_zlo_kernel, [spread[2:]] * YC, [VMEM] * ZLO, limit=SMALL)(*parts)
    (rows,) = local(
        rows_kernel,
        [(blocks, vecs, LANE)],
        [SMEM] * 3 + [HBM, VMEM, VMEM, VMEM],
        tile_scratch(REGIONS * blocks, None),
        ROWS,
        half,
    )(*ids, tile_set, own, far, mine)
    rows, *parts = lax.optimization_barrier((rows, *parts))
    rows = exchange(rows, GRP_AXES)
    parts = swaps(parts, YC_AXES, YC)
    (total,) = local(final_kernel, [(vecs, LANE)], [SMEM] + [VMEM] * (1 + YC), limit=SMALL)(
        yc, rows, *parts
    )
    return total[None]


def solution(mesh):
    fine = Mesh(mesh.devices.reshape(ZLO, X, ZHI, Y, CORE), ("zlo", "x", "zhi", "y", "core"))
    return jax.shard_map(
        on_device,
        mesh=fine,
        in_specs=(
            P(OWN_AXES, None, None),
            P(GRP_AXES, OWN_AXES, None, None, None),
            P(GRP_AXES, OWN_AXES, None),
            P(GRP_AXES, OWN_AXES, None),
            P(GRP_AXES, OWN_AXES),
            P(GRP_AXES, None),
        ),
        out_specs=P(OWN_AXES, None, GRP_AXES),
        check_vma=False,
    )
```

```python
import jax
import jax.numpy as jnp
from jax import lax
from jax.experimental import pallas as pl
from jax.experimental.pallas import tpu as pltpu
from jax.sharding import Mesh, PartitionSpec as P

ZLO, X, ZHI, Y, CORE = 4, 4, 2, 4, 2
YC = Y * CORE
OWN = ZHI * YC
FAN = X * YC
GRP_AXES = ("zlo", "x")
OWN_AXES = ("zhi", "y", "core")
FAN_AXES = ("x", "y", "core")
YC_AXES = ("y", "core")


REGIONS = 4
SUB = 8
LANE = 128
CHUNK = 32
GROUPS = (32, 8, 1)
SMALL = 8 << 20
LARGE = 56 << 20
ROWS = 52 << 20

VMEM = pl.BlockSpec(memory_space=pltpu.VMEM)
SMEM = pl.BlockSpec(memory_space=pltpu.SMEM)
HBM = pl.BlockSpec(memory_space=pltpu.HBM)

BY_COLS = (((1,), (0,)), ((), ()))
BY_ROWS = (((1,), (1,)), ((), ()))


def halves(value):
    high = value.astype(jnp.bfloat16)
    return high, (value - high.astype(jnp.float32)).astype(jnp.bfloat16)


def dot(left, right, dims):
    return lax.dot_general(left, right, dims, preferred_element_type=jnp.float32)


def by_columns(pair, high, low):
    count = pair.shape[0] // 2
    wide = dot(pair, jnp.concatenate([high, low], axis=1), BY_COLS)
    return wide[:count, :LANE] + wide[count:, :LANE] + wide[:count, LANE:]


def by_rows(pair, high, low):
    count = pair.shape[0] // 2
    top = jnp.concatenate([pair[:count], pair[:count]], axis=1)
    bottom = jnp.concatenate([pair[count:], jnp.zeros_like(pair[count:])], axis=1)
    tall = dot(
        jnp.concatenate([top, bottom], axis=0), jnp.concatenate([high, low], axis=1), BY_ROWS
    )
    return tall[:count] + tall[count:]


def pieces_kernel(x_ref, yc_ref, own_ref, out_ref, held, sems):
    copies = []
    for zlo in range(ZLO):
        col = pl.multiple_of((zlo * X + x_ref[0]) * LANE, LANE)
        copies.append(
            pltpu.make_async_copy(own_ref.at[:, pl.ds(col, LANE)], held.at[zlo], sems.at[zlo])
        )
    for copy in copies:
        copy.start()
    for copy in copies:
        copy.wait()
    for step in range(YC):
        row = pl.multiple_of((yc_ref[0] ^ step) * SUB, SUB)
        for zlo in range(ZLO):
            out_ref[step, zlo] = held[zlo, pl.ds(row, SUB)]


def pair_kernel(near_ref, other_ref, *outs):
    for step in range(YC):
        outs[step][0] = near_ref[step]
        outs[step][1] = other_ref[step]


def route_kernel(x_ref, yc_ref, m0, m1, m2, m3, *refs):
    pieces, out_ref, held = refs[:YC], refs[YC], refs[YC + 1]
    for step in range(YC):
        for zhi in range(ZHI):
            held[zhi * YC + step] = pieces[step][zhi]
    for step, masks in enumerate((m0, m1, m2, m3)):
        base = lax.rem(x_ref[0] + step, X) * YC
        for slot in range(REGIONS - 1):
            mask = masks[0, slot]
            for part in range(YC):
                out_ref[base + part, slot] = held[(part ^ yc_ref[0]) ^ mask]


def collect_kernel(x_ref, yc_ref, zlo_ref, m0, m1, m2, m3, parts_ref, near_ref, other_ref, sums):
    sums[...] = jnp.zeros_like(sums)
    for step, masks in enumerate((m0, m1, m2, m3)):
        base = lax.rem(x_ref[0] + step, X) * YC
        for slot in range(REGIONS - 1):
            mask = masks[0, slot]
            for part in range(YC):
                owner = (part ^ yc_ref[0]) ^ mask
                for zlo in range(ZLO):
                    sums[zlo, owner] += parts_ref[base + part, slot, zlo]
    for step in range(ZLO):
        zlo = zlo_ref[0] ^ step
        near_ref[step] = sums[zlo, :YC]
        other_ref[step] = sums[zlo, YC:]


def add_zhi_kernel(a_ref, b_ref, *outs):
    for step in range(ZLO):
        outs[step][...] = a_ref[step] + b_ref[step]


def add_zlo_kernel(a_ref, b_ref, c_ref, d_ref, *outs):
    for step in range(YC):
        outs[step][...] = (a_ref[step] + b_ref[step]) + (c_ref[step] + d_ref[step])


def final_kernel(yc_ref, rows_ref, *refs):
    parts, out_ref = refs[:YC], refs[YC]
    for step in range(YC):
        at = pl.ds(pl.multiple_of((yc_ref[0] ^ step) * SUB, SUB), SUB)
        total = parts[step][...]
        for group in range(rows_ref.shape[0]):
            total = total + rows_ref[group, at]
        out_ref[at] = total


def load_table(table, base, blocks, get, vecs):
    for block in range(blocks):
        high, low = halves(get(block))
        table[base + block, :vecs] = high
        table[base + block, vecs:] = low


def fetch(tiles, held, sems):
    copies = [
        pltpu.make_async_copy(
            tiles.at[pl.ds(i * CHUNK, CHUNK)], held.at[pl.ds(i * CHUNK, CHUNK)], sems.at[i]
        )
        for i in range(held.shape[0] // CHUNK)
    ]
    for copy in copies:
        copy.start()
    return copies


def each_group(copies, live, group):
    for i, copy in enumerate(copies):
        copy.wait()
        done = 0
        here = jnp.clip(live - i * CHUNK, 0, CHUNK)
        for size in GROUPS:

            def step(at, carry, i=i, size=size):
                group(i * CHUNK + at * size, size)
                return carry

            lax.fori_loop(done // size, here // size, step, 0)
            done = here // size * size


def columns_kernel(rows, cols, count, tiles, own, out_ref, self_ref, held, table, sums, near, sems):
    first = pltpu.make_async_copy(own, near, sems.at[sems.shape[0] - 1])
    first.start()
    copies = fetch(tiles, held, sems)
    sums[...] = jnp.zeros_like(sums)
    vecs = near.shape[0]
    blocks = near.shape[1] // LANE
    first.wait()
    load_table(table, 0, blocks, lambda b: near[:, b * LANE : (b + 1) * LANE], vecs)

    def group(first, size):
        done = []
        for k in range(size):
            done.append(by_columns(table[rows[first + k]], *halves(held[first + k])))
        for k in range(size):
            col = cols[first + k]
            sums[col] += done[k]

    each_group(copies, count[0], group)
    self_ref[...] = sums[:blocks]
    for slot in range(REGIONS - 1):
        for block in range(blocks):
            zlo, x = divmod(block, X)
            value = sums[(slot + 1) * blocks + block]
            for part in range(YC):
                out_ref[x * YC + part, slot, zlo] = value[part * SUB : (part + 1) * SUB]


def rows_kernel(
    rows, cols, count, tiles, own, far, mine, sums, held, table, near, away, sems
):
    last = sems.shape[0] - 3
    operands = [
        pltpu.make_async_copy(source, target, sems.at[last + i])
        for i, (source, target) in enumerate(((own, near), (far, away), (mine, sums)))
    ]
    for copy in operands:
        copy.start()
    copies = fetch(tiles, held, sems)
    vecs = near.shape[0]
    blocks = near.shape[1] // LANE
    operands[0].wait()
    load_table(table, 0, blocks, lambda b: near[:, b * LANE : (b + 1) * LANE], vecs)
    operands[1].wait()
    for slot in range(REGIONS - 1):

        def piece(b, slot=slot):
            return jnp.concatenate(
                [away[b % X * YC + part, slot, b // X] for part in range(YC)], axis=0
            )

        load_table(table, (slot + 1) * blocks, blocks, piece, vecs)
    operands[2].wait()

    def group(first, size):
        done = []
        for k in range(size):
            done.append(by_rows(table[cols[first + k]], *halves(held[first + k])))
        for k in range(size):
            row = rows[first + k]
            sums[row] += done[k]

    each_group(copies, count[0], group)


def exchange(value, axes):
    return lax.all_to_all(value, axes, 0, 0, tiled=False)


def local(kernel, outs, specs, scratch=(), limit=None, cost=None):
    outs = [jax.ShapeDtypeStruct(shape, jnp.float32) for shape in outs]
    return pl.pallas_call(
        kernel,
        out_shape=outs,
        in_specs=specs,
        out_specs=[VMEM] * len(outs),
        scratch_shapes=scratch,
        compiler_params=pltpu.CompilerParams(vmem_limit_bytes=limit),
        cost_estimate=cost,
    )


def swaps(arrays, axes, count):
    return [arrays[0]] + [
        lax.ppermute(arrays[step], axes, [(i, i ^ step) for i in range(count)])
        for step in range(1, count)
    ]


def on_device(vectors, tiles, tile_rows, tile_cols, tile_counts, matchings):
    own = vectors[0]
    tile_set = tiles[0, 0]
    vecs, rows_own = own.shape
    slots = tile_set.shape[0]
    blocks = rows_own // LANE
    x, zlo, yc = (
        lax.axis_index(axes).reshape(1).astype(jnp.int32) for axes in ("x", "zlo", YC_AXES)
    )
    ids = (tile_rows[0, 0], tile_cols[0, 0], tile_counts[0])
    piece = (ZLO, SUB, LANE)
    half = pl.CostEstimate(
        flops=slots * 6 * vecs * LANE * LANE, bytes_accessed=tile_set.size * 4, transcendentals=0
    )

    def tile_scratch(operand, extra, copies):
        return [
            pltpu.VMEM(tile_set.shape, jnp.float32),
            pltpu.VMEM((operand, 2 * vecs, LANE), jnp.bfloat16),
            *(pltpu.VMEM(shape, jnp.float32) for shape in extra),
            pltpu.SemaphoreType.DMA((slots // CHUNK + copies,)),
        ]

    whole = (YC, *piece)
    (near,) = local(
        pieces_kernel,
        [whole],
        [SMEM] * 2 + [HBM],
        [pltpu.VMEM((ZLO, vecs, LANE), jnp.float32), pltpu.SemaphoreType.DMA((ZLO,))],
        SMALL,
    )(x, yc, own)
    other = lax.ppermute(near, "zhi", [(0, 1), (1, 0)])
    masks = [matchings] + [
        lax.ppermute(matchings, "x", [(i, (i - step) % X) for i in range(X)])
        for step in range(1, X)
    ]
    parts, mine = local(
        columns_kernel,
        [(FAN, REGIONS - 1, *piece), (blocks, vecs, LANE)],
        [SMEM] * 3 + [HBM] * 2,
        tile_scratch(blocks, [(REGIONS * blocks, vecs, LANE), own.shape], 1),
        LARGE,
        half,
    )(*ids, tile_set, own)
    parts = exchange(parts, FAN_AXES)
    pieces = local(pair_kernel, [(ZHI, *piece)] * YC, [VMEM] * 2, limit=SMALL)(near, other)
    pieces = swaps(pieces, YC_AXES, YC)
    (wanted,) = local(
        route_kernel,
        [(FAN, REGIONS - 1, *piece)],
        [SMEM] * 6 + [VMEM] * YC,
        [pltpu.VMEM((OWN, *piece), jnp.float32)],
        SMALL,
    )(x, yc, *masks, *pieces)
    parts, wanted = lax.optimization_barrier((parts, wanted))
    far = exchange(wanted, FAN_AXES)
    spread = (ZLO, YC, SUB, LANE)
    near, other = local(
        collect_kernel,
        [spread] * 2,
        [SMEM] * 7 + [VMEM],
        [pltpu.VMEM((ZLO, OWN, SUB, LANE), jnp.float32)],
        SMALL,
    )(x, yc, zlo, *masks, parts)
    other = lax.ppermute(other, "zhi", [(0, 1), (1, 0)])
    parts = local(add_zhi_kernel, [spread[1:]] * ZLO, [VMEM] * 2, limit=SMALL)(near, other)
    parts = swaps(parts, "zlo", ZLO)
    parts = local(add_zlo_kernel, [spread[2:]] * YC, [VMEM] * ZLO, limit=SMALL)(*parts)
    (rows,) = local(
        rows_kernel,
        [(blocks, vecs, LANE)],
        [SMEM] * 3 + [HBM] * 4,
        tile_scratch(REGIONS * blocks, [own.shape, wanted.shape], 3),
        ROWS,
        half,
    )(*ids, tile_set, own, far, mine)
    rows, *parts = lax.optimization_barrier((rows, *parts))
    rows = exchange(rows, GRP_AXES)
    parts = swaps(parts, YC_AXES, YC)
    (total,) = local(final_kernel, [(vecs, LANE)], [SMEM] + [VMEM] * (1 + YC), limit=SMALL)(
        yc, rows, *parts
    )
    return total[None]


def solution(mesh):
    fine = Mesh(mesh.devices.reshape(ZLO, X, ZHI, Y, CORE), ("zlo", "x", "zhi", "y", "core"))
    return jax.shard_map(
        on_device,
        mesh=fine,
        in_specs=(
            P(OWN_AXES, None, None),
            P(GRP_AXES, OWN_AXES, None, None, None),
            P(GRP_AXES, OWN_AXES, None),
            P(GRP_AXES, OWN_AXES, None),
            P(GRP_AXES, OWN_AXES),
            P(GRP_AXES, None),
        ),
        out_specs=P(OWN_AXES, None, GRP_AXES),
        check_vma=False,
    )
```

```python
import jax
import jax.numpy as jnp
from jax import lax
from jax.experimental import pallas as pl
from jax.experimental.pallas import tpu as pltpu
from jax.sharding import Mesh, PartitionSpec as P

ZLO, X, ZHI, Y, CORE = 4, 4, 2, 4, 2
YC = Y * CORE
OWN = ZHI * YC
FAN = X * YC
GRP_AXES = ("zlo", "x")
OWN_AXES = ("zhi", "y", "core")
FAN_AXES = ("x", "y", "core")
YC_AXES = ("y", "core")


REGIONS = 4
SUB = 8
LANE = 128
CHUNK = 32
GROUPS = (32, 8, 1)
SMALL = 8 << 20
LARGE = 56 << 20
ROWS = 52 << 20

VMEM = pl.BlockSpec(memory_space=pltpu.VMEM)
SMEM = pl.BlockSpec(memory_space=pltpu.SMEM)
HBM = pl.BlockSpec(memory_space=pltpu.HBM)

BY_COLS = (((1,), (0,)), ((), ()))
BY_ROWS = (((1,), (1,)), ((), ()))


def halves(value):
    high = value.astype(jnp.bfloat16)
    return high, (value - high.astype(jnp.float32)).astype(jnp.bfloat16)


def dot(left, right, dims):
    return lax.dot_general(left, right, dims, preferred_element_type=jnp.float32)


def by_columns(pair, high, low):
    count = pair.shape[0] // 2
    wide = dot(pair, jnp.concatenate([high, low], axis=1), BY_COLS)
    return wide[:count, :LANE] + wide[count:, :LANE] + wide[:count, LANE:]


def by_rows(pair, high, low):
    count = pair.shape[0] // 2
    top = jnp.concatenate([pair[:count], pair[:count]], axis=1)
    bottom = jnp.concatenate([pair[count:], jnp.zeros_like(pair[count:])], axis=1)
    tall = dot(
        jnp.concatenate([top, bottom], axis=0), jnp.concatenate([high, low], axis=1), BY_ROWS
    )
    return tall[:count] + tall[count:]


def pieces_kernel(x_ref, yc_ref, own_ref, out_ref, held, sems):
    copies = []
    for zlo in range(ZLO):
        col = pl.multiple_of((zlo * X + x_ref[0]) * LANE, LANE)
        copies.append(
            pltpu.make_async_copy(own_ref.at[:, pl.ds(col, LANE)], held.at[zlo], sems.at[zlo])
        )
    for copy in copies:
        copy.start()
    for copy in copies:
        copy.wait()
    for step in range(YC):
        row = pl.multiple_of((yc_ref[0] ^ step) * SUB, SUB)
        for zlo in range(ZLO):
            out_ref[step, zlo] = held[zlo, pl.ds(row, SUB)]


def pair_kernel(near_ref, other_ref, same_ref, cross_ref):
    for step in range(Y):
        for core, out_ref in enumerate((same_ref, cross_ref)):
            out_ref[step, 0] = near_ref[step * CORE + core]
            out_ref[step, 1] = other_ref[step * CORE + core]


def join_kernel(same_ref, cross_ref, *outs):
    for step in range(Y):
        outs[step][0] = same_ref[step]
        outs[step][1] = cross_ref[step]


def route_kernel(x_ref, yc_ref, m0, m1, m2, m3, *refs):
    pieces, out_ref, held = refs[:Y], refs[Y], refs[Y + 1]
    for step in range(Y):
        for core in range(CORE):
            for zhi in range(ZHI):
                held[zhi * YC + step * CORE + core] = pieces[step][core, zhi]
    for step, masks in enumerate((m0, m1, m2, m3)):
        base = lax.rem(x_ref[0] + step, X) * YC
        for slot in range(REGIONS - 1):
            mask = masks[0, slot]
            for part in range(YC):
                out_ref[base + part, slot] = held[(part ^ yc_ref[0]) ^ mask]


def collect_kernel(x_ref, yc_ref, zlo_ref, m0, m1, m2, m3, parts_ref, near_ref, other_ref, sums):
    sums[...] = jnp.zeros_like(sums)
    for step, masks in enumerate((m0, m1, m2, m3)):
        base = lax.rem(x_ref[0] + step, X) * YC
        for slot in range(REGIONS - 1):
            mask = masks[0, slot]
            for part in range(YC):
                owner = (part ^ yc_ref[0]) ^ mask
                for zlo in range(ZLO):
                    sums[zlo, owner] += parts_ref[base + part, slot, zlo]
    for step in range(ZLO):
        zlo = zlo_ref[0] ^ step
        near_ref[step] = sums[zlo, :YC]
        other_ref[step] = sums[zlo, YC:]


def add_zhi_kernel(a_ref, b_ref, *outs):
    for step in range(ZLO):
        outs[step][...] = a_ref[step] + b_ref[step]


def add_zlo_kernel(a_ref, b_ref, c_ref, d_ref, *outs):
    for step in range(YC):
        outs[step][...] = (a_ref[step] + b_ref[step]) + (c_ref[step] + d_ref[step])


def final_kernel(yc_ref, rows_ref, *refs):
    parts, out_ref = refs[:YC], refs[YC]
    for step in range(YC):
        at = pl.ds(pl.multiple_of((yc_ref[0] ^ step) * SUB, SUB), SUB)
        total = parts[step][...]
        for group in range(rows_ref.shape[0]):
            total = total + rows_ref[group, at]
        out_ref[at] = total


def load_table(table, base, blocks, get, vecs):
    for block in range(blocks):
        high, low = halves(get(block))
        table[base + block, :vecs] = high
        table[base + block, vecs:] = low


def fetch(tiles, held, sems):
    copies = [
        pltpu.make_async_copy(
            tiles.at[pl.ds(i * CHUNK, CHUNK)], held.at[pl.ds(i * CHUNK, CHUNK)], sems.at[i]
        )
        for i in range(held.shape[0] // CHUNK)
    ]
    for copy in copies:
        copy.start()
    return copies


def each_group(copies, live, group):
    for i, copy in enumerate(copies):
        copy.wait()
        done = 0
        here = jnp.clip(live - i * CHUNK, 0, CHUNK)
        for size in GROUPS:

            def step(at, carry, i=i, size=size):
                group(i * CHUNK + at * size, size)
                return carry

            lax.fori_loop(done // size, here // size, step, 0)
            done = here // size * size


def columns_kernel(rows, cols, count, tiles, own, out_ref, self_ref, held, table, sums, near, sems):
    first = pltpu.make_async_copy(own, near, sems.at[sems.shape[0] - 1])
    first.start()
    copies = fetch(tiles, held, sems)
    sums[...] = jnp.zeros_like(sums)
    vecs = near.shape[0]
    blocks = near.shape[1] // LANE
    first.wait()
    load_table(table, 0, blocks, lambda b: near[:, b * LANE : (b + 1) * LANE], vecs)

    def group(first, size):
        done = []
        for k in range(size):
            done.append(by_columns(table[rows[first + k]], *halves(held[first + k])))
        for k in range(size):
            col = cols[first + k]
            sums[col] += done[k]

    each_group(copies, count[0], group)
    self_ref[...] = sums[:blocks]
    for slot in range(REGIONS - 1):
        for block in range(blocks):
            zlo, x = divmod(block, X)
            value = sums[(slot + 1) * blocks + block]
            for part in range(YC):
                out_ref[x * YC + part, slot, zlo] = value[part * SUB : (part + 1) * SUB]


def rows_kernel(
    rows, cols, count, tiles, own, far, mine, sums, held, table, near, away, sems
):
    last = sems.shape[0] - 3
    operands = [
        pltpu.make_async_copy(source, target, sems.at[last + i])
        for i, (source, target) in enumerate(((own, near), (far, away), (mine, sums)))
    ]
    for copy in operands:
        copy.start()
    copies = fetch(tiles, held, sems)
    vecs = near.shape[0]
    blocks = near.shape[1] // LANE
    operands[0].wait()
    load_table(table, 0, blocks, lambda b: near[:, b * LANE : (b + 1) * LANE], vecs)
    operands[1].wait()
    for slot in range(REGIONS - 1):

        def piece(b, slot=slot):
            return jnp.concatenate(
                [away[b % X * YC + part, slot, b // X] for part in range(YC)], axis=0
            )

        load_table(table, (slot + 1) * blocks, blocks, piece, vecs)
    operands[2].wait()

    def group(first, size):
        done = []
        for k in range(size):
            done.append(by_rows(table[cols[first + k]], *halves(held[first + k])))
        for k in range(size):
            row = rows[first + k]
            sums[row] += done[k]

    each_group(copies, count[0], group)


def exchange(value, axes):
    return lax.all_to_all(value, axes, 0, 0, tiled=False)


def local(kernel, outs, specs, scratch=(), limit=None, cost=None):
    outs = [jax.ShapeDtypeStruct(shape, jnp.float32) for shape in outs]
    return pl.pallas_call(
        kernel,
        out_shape=outs,
        in_specs=specs,
        out_specs=[VMEM] * len(outs),
        scratch_shapes=scratch,
        compiler_params=pltpu.CompilerParams(vmem_limit_bytes=limit),
        cost_estimate=cost,
    )


def swaps(arrays, axes, count):
    return [arrays[0]] + [
        lax.ppermute(arrays[step], axes, [(i, i ^ step) for i in range(count)])
        for step in range(1, count)
    ]


def on_device(vectors, tiles, tile_rows, tile_cols, tile_counts, matchings):
    own = vectors[0]
    tile_set = tiles[0, 0]
    vecs, rows_own = own.shape
    slots = tile_set.shape[0]
    blocks = rows_own // LANE
    x, zlo, yc = (
        lax.axis_index(axes).reshape(1).astype(jnp.int32) for axes in ("x", "zlo", YC_AXES)
    )
    ids = (tile_rows[0, 0], tile_cols[0, 0], tile_counts[0])
    piece = (ZLO, SUB, LANE)
    half = pl.CostEstimate(
        flops=slots * 6 * vecs * LANE * LANE, bytes_accessed=tile_set.size * 4, transcendentals=0
    )

    def tile_scratch(operand, extra, copies):
        return [
            pltpu.VMEM(tile_set.shape, jnp.float32),
            pltpu.VMEM((operand, 2 * vecs, LANE), jnp.bfloat16),
            *(pltpu.VMEM(shape, jnp.float32) for shape in extra),
            pltpu.SemaphoreType.DMA((slots // CHUNK + copies,)),
        ]

    whole = (YC, *piece)
    (near,) = local(
        pieces_kernel,
        [whole],
        [SMEM] * 2 + [HBM],
        [pltpu.VMEM((ZLO, vecs, LANE), jnp.float32), pltpu.SemaphoreType.DMA((ZLO,))],
        SMALL,
    )(x, yc, own)
    other = lax.ppermute(near, ("zlo", "zhi"), [(i, ZLO * ZHI - 1 - i) for i in range(ZLO * ZHI)])
    masks = [matchings] + [
        lax.ppermute(matchings, "x", [(i, (i - step) % X) for i in range(X)])
        for step in range(1, X)
    ]
    parts, mine = local(
        columns_kernel,
        [(FAN, REGIONS - 1, *piece), (blocks, vecs, LANE)],
        [SMEM] * 3 + [HBM] * 2,
        tile_scratch(blocks, [(REGIONS * blocks, vecs, LANE), own.shape], 1),
        LARGE,
        half,
    )(*ids, tile_set, own)
    parts = exchange(parts, FAN_AXES)
    side = (Y, ZHI, *piece)
    same, cross = local(pair_kernel, [side] * CORE, [VMEM] * 2, limit=SMALL)(near, other)
    cross = lax.ppermute(cross, "core", [(0, 1), (1, 0)])
    pieces = local(join_kernel, [(CORE, ZHI, *piece)] * Y, [VMEM] * 2, limit=SMALL)(same, cross)
    pieces = swaps(pieces, "y", Y)
    (wanted,) = local(
        route_kernel,
        [(FAN, REGIONS - 1, *piece)],
        [SMEM] * 6 + [VMEM] * Y,
        [pltpu.VMEM((OWN, *piece), jnp.float32)],
        SMALL,
    )(x, yc, *masks, *pieces)
    parts, wanted = lax.optimization_barrier((parts, wanted))
    far = exchange(wanted, FAN_AXES)
    spread = (ZLO, YC, SUB, LANE)
    near, other = local(
        collect_kernel,
        [spread] * 2,
        [SMEM] * 7 + [VMEM],
        [pltpu.VMEM((ZLO, OWN, SUB, LANE), jnp.float32)],
        SMALL,
    )(x, yc, zlo, *masks, parts)
    other = lax.ppermute(other, "zhi", [(0, 1), (1, 0)])
    parts = local(add_zhi_kernel, [spread[1:]] * ZLO, [VMEM] * 2, limit=SMALL)(near, other)
    parts = swaps(parts, "zlo", ZLO)
    parts = local(add_zlo_kernel, [spread[2:]] * YC, [VMEM] * ZLO, limit=SMALL)(*parts)
    (rows,) = local(
        rows_kernel,
        [(blocks, vecs, LANE)],
        [SMEM] * 3 + [HBM] * 4,
        tile_scratch(REGIONS * blocks, [own.shape, wanted.shape], 3),
        ROWS,
        half,
    )(*ids, tile_set, own, far, mine)
    rows, *parts = lax.optimization_barrier((rows, *parts))
    rows = exchange(rows, GRP_AXES)
    parts = swaps(parts, YC_AXES, YC)
    (total,) = local(final_kernel, [(vecs, LANE)], [SMEM] + [VMEM] * (1 + YC), limit=SMALL)(
        yc, rows, *parts
    )
    return total[None]


def solution(mesh):
    fine = Mesh(mesh.devices.reshape(ZLO, X, ZHI, Y, CORE), ("zlo", "x", "zhi", "y", "core"))
    return jax.shard_map(
        on_device,
        mesh=fine,
        in_specs=(
            P(OWN_AXES, None, None),
            P(GRP_AXES, OWN_AXES, None, None, None),
            P(GRP_AXES, OWN_AXES, None),
            P(GRP_AXES, OWN_AXES, None),
            P(GRP_AXES, OWN_AXES),
            P(GRP_AXES, None),
        ),
        out_specs=P(OWN_AXES, None, GRP_AXES),
        check_vma=False,
    )
```

```python
import jax
import jax.numpy as jnp
from jax import lax
from jax.experimental import pallas as pl
from jax.experimental.pallas import tpu as pltpu
from jax.sharding import Mesh, PartitionSpec as P

ZLO, X, ZHI, Y, CORE = 4, 4, 2, 4, 2
YC = Y * CORE
OWN = ZHI * YC
FAN = X * YC
GRP_AXES = ("zlo", "x")
OWN_AXES = ("zhi", "y", "core")
FAN_AXES = ("x", "y", "core")
YC_AXES = ("y", "core")


REGIONS = 4
SUB = 8
LANE = 128
CHUNK = 32
GROUPS = (32, 8, 1)
SMALL = 8 << 20
LARGE = 56 << 20
ROWS = 52 << 20

VMEM = pl.BlockSpec(memory_space=pltpu.VMEM)
SMEM = pl.BlockSpec(memory_space=pltpu.SMEM)
HBM = pl.BlockSpec(memory_space=pltpu.HBM)

BY_COLS = (((1,), (0,)), ((), ()))
BY_ROWS = (((1,), (1,)), ((), ()))


def halves(value):
    high = value.astype(jnp.bfloat16)
    return high, (value - high.astype(jnp.float32)).astype(jnp.bfloat16)


def dot(left, right, dims):
    return lax.dot_general(left, right, dims, preferred_element_type=jnp.float32)


def by_columns(pair, high, low):
    count = pair.shape[0] // 2
    wide = dot(pair, jnp.concatenate([high, low], axis=1), BY_COLS)
    return wide[:count, :LANE] + wide[count:, :LANE] + wide[:count, LANE:]


def by_rows(pair, high, low):
    count = pair.shape[0] // 2
    top = jnp.concatenate([pair[:count], pair[:count]], axis=1)
    bottom = jnp.concatenate([pair[count:], jnp.zeros_like(pair[count:])], axis=1)
    tall = dot(
        jnp.concatenate([top, bottom], axis=0), jnp.concatenate([high, low], axis=1), BY_ROWS
    )
    return tall[:count] + tall[count:]


def pieces_kernel(x_ref, yc_ref, own_ref, out_ref, held, sems):
    copies = []
    for zlo in range(ZLO):
        col = pl.multiple_of((zlo * X + x_ref[0]) * LANE, LANE)
        copies.append(
            pltpu.make_async_copy(own_ref.at[:, pl.ds(col, LANE)], held.at[zlo], sems.at[zlo])
        )
    for copy in copies:
        copy.start()
    for copy in copies:
        copy.wait()
    for step in range(YC):
        row = pl.multiple_of((yc_ref[0] ^ step) * SUB, SUB)
        for zlo in range(ZLO):
            out_ref[step, zlo] = held[zlo, pl.ds(row, SUB)]


def pair_kernel(near_ref, other_ref, same_ref, cross_ref):
    for step in range(Y):
        for core, out_ref in enumerate((same_ref, cross_ref)):
            out_ref[step, 0] = near_ref[step * CORE + core]
            out_ref[step, 1] = other_ref[step * CORE + core]


def join_kernel(same_ref, cross_ref, *outs):
    for step in range(Y):
        outs[step][0] = same_ref[step]
        outs[step][1] = cross_ref[step]


def route_kernel(x_ref, yc_ref, m0, m1, m2, m3, *refs):
    pieces, (out, held, out_ref, sems) = refs[:Y], refs[Y:]
    for step in range(Y):
        for core in range(CORE):
            for zhi in range(ZHI):
                held[zhi * YC + step * CORE + core] = pieces[step][core, zhi]
    results = []
    for step, masks in enumerate((m0, m1, m2, m3)):
        base = lax.rem(x_ref[0] + step, X) * YC
        for slot in range(REGIONS - 1):
            mask = masks[0, slot]
            for part in range(YC):
                out_ref[base + part, slot] = held[(part ^ yc_ref[0]) ^ mask]
        here = pl.ds(base, YC)
        results.append(pltpu.make_async_copy(out_ref.at[here], out.at[here], sems.at[step]))
        results[-1].start()
    for copy in results:
        copy.wait()


def collect_kernel(x_ref, yc_ref, zlo_ref, m0, m1, m2, m3, parts_ref, near_ref, other_ref, sums):
    sums[...] = jnp.zeros_like(sums)
    for step, masks in enumerate((m0, m1, m2, m3)):
        base = lax.rem(x_ref[0] + step, X) * YC
        for slot in range(REGIONS - 1):
            mask = masks[0, slot]
            for part in range(YC):
                owner = (part ^ yc_ref[0]) ^ mask
                for zlo in range(ZLO):
                    sums[zlo, owner] += parts_ref[base + part, slot, zlo]
    for step in range(ZLO):
        zlo = zlo_ref[0] ^ step
        near_ref[step] = sums[zlo, :YC]
        other_ref[step] = sums[zlo, YC:]


def add_zhi_kernel(a_ref, b_ref, *outs):
    for step in range(ZLO):
        outs[step][...] = a_ref[step] + b_ref[step]


def add_zlo_kernel(a_ref, b_ref, c_ref, d_ref, *outs):
    for step in range(YC):
        outs[step][...] = (a_ref[step] + b_ref[step]) + (c_ref[step] + d_ref[step])


def final_kernel(yc_ref, rows_ref, *refs):
    parts, out_ref = refs[:YC], refs[YC]
    for step in range(YC):
        at = pl.ds(pl.multiple_of((yc_ref[0] ^ step) * SUB, SUB), SUB)
        total = parts[step][...]
        for group in range(rows_ref.shape[0]):
            total = total + rows_ref[group, at]
        out_ref[at] = total


def load_table(table, base, blocks, get, vecs):
    for block in range(blocks):
        high, low = halves(get(block))
        table[base + block, :vecs] = high
        table[base + block, vecs:] = low


def fetch(tiles, held, sems):
    copies = [
        pltpu.make_async_copy(
            tiles.at[pl.ds(i * CHUNK, CHUNK)], held.at[pl.ds(i * CHUNK, CHUNK)], sems.at[i]
        )
        for i in range(held.shape[0] // CHUNK)
    ]
    for copy in copies:
        copy.start()
    return copies


def each_group(copies, live, group):
    for i, copy in enumerate(copies):
        copy.wait()
        done = 0
        here = jnp.clip(live - i * CHUNK, 0, CHUNK)
        for size in GROUPS:

            def step(at, carry, i=i, size=size):
                group(i * CHUNK + at * size, size)
                return carry

            lax.fori_loop(done // size, here // size, step, 0)
            done = here // size * size


def columns_kernel(
    rows, cols, count, tiles, own, out, self_out, held, table, sums, near, out_ref, sems, out_sems
):
    first = pltpu.make_async_copy(own, near, sems.at[sems.shape[0] - 1])
    first.start()
    copies = fetch(tiles, held, sems)
    sums[...] = jnp.zeros_like(sums)
    vecs = near.shape[0]
    blocks = near.shape[1] // LANE
    first.wait()
    load_table(table, 0, blocks, lambda b: near[:, b * LANE : (b + 1) * LANE], vecs)

    def group(first, size):
        done = []
        for k in range(size):
            done.append(by_columns(table[rows[first + k]], *halves(held[first + k])))
        for k in range(size):
            col = cols[first + k]
            sums[col] += done[k]

    each_group(copies, count[0], group)
    mine = pltpu.make_async_copy(sums.at[pl.ds(0, blocks)], self_out, out_sems.at[X])
    mine.start()
    results = []
    for x in range(X):
        here = pl.ds(x * YC, YC)
        for slot in range(REGIONS - 1):
            for zlo in range(blocks // X):
                value = sums[(slot + 1) * blocks + zlo * X + x]
                for part in range(YC):
                    out_ref[x * YC + part, slot, zlo] = value[part * SUB : (part + 1) * SUB]
        results.append(pltpu.make_async_copy(out_ref.at[here], out.at[here], out_sems.at[x]))
        results[-1].start()
    for copy in (mine, *results):
        copy.wait()


def rows_kernel(
    rows, cols, count, tiles, own, far, mine, sums, held, table, near, away, sems
):
    last = sems.shape[0] - 3
    operands = [
        pltpu.make_async_copy(source, target, sems.at[last + i])
        for i, (source, target) in enumerate(((own, near), (far, away), (mine, sums)))
    ]
    for copy in operands:
        copy.start()
    copies = fetch(tiles, held, sems)
    vecs = near.shape[0]
    blocks = near.shape[1] // LANE
    operands[0].wait()
    load_table(table, 0, blocks, lambda b: near[:, b * LANE : (b + 1) * LANE], vecs)
    operands[1].wait()
    for slot in range(REGIONS - 1):

        def piece(b, slot=slot):
            return jnp.concatenate(
                [away[b % X * YC + part, slot, b // X] for part in range(YC)], axis=0
            )

        load_table(table, (slot + 1) * blocks, blocks, piece, vecs)
    operands[2].wait()

    def group(first, size):
        done = []
        for k in range(size):
            done.append(by_rows(table[cols[first + k]], *halves(held[first + k])))
        for k in range(size):
            row = rows[first + k]
            sums[row] += done[k]

    each_group(copies, count[0], group)


def exchange(value, axes):
    return lax.all_to_all(value, axes, 0, 0, tiled=False)


def local(kernel, outs, specs, scratch=(), limit=None, cost=None, place=VMEM):
    outs = [jax.ShapeDtypeStruct(shape, jnp.float32) for shape in outs]
    return pl.pallas_call(
        kernel,
        out_shape=outs,
        in_specs=specs,
        out_specs=[place] * len(outs),
        scratch_shapes=scratch,
        compiler_params=pltpu.CompilerParams(vmem_limit_bytes=limit),
        cost_estimate=cost,
    )


def swaps(arrays, axes, count):
    return [arrays[0]] + [
        lax.ppermute(arrays[step], axes, [(i, i ^ step) for i in range(count)])
        for step in range(1, count)
    ]


def on_device(vectors, tiles, tile_rows, tile_cols, tile_counts, matchings):
    own = vectors[0]
    tile_set = tiles[0, 0]
    vecs, rows_own = own.shape
    slots = tile_set.shape[0]
    blocks = rows_own // LANE
    x, zlo, yc = (
        lax.axis_index(axes).reshape(1).astype(jnp.int32) for axes in ("x", "zlo", YC_AXES)
    )
    ids = (tile_rows[0, 0], tile_cols[0, 0], tile_counts[0])
    piece = (ZLO, SUB, LANE)
    half = pl.CostEstimate(
        flops=slots * 6 * vecs * LANE * LANE, bytes_accessed=tile_set.size * 4, transcendentals=0
    )

    def tile_scratch(operand, extra, copies):
        return [
            pltpu.VMEM(tile_set.shape, jnp.float32),
            pltpu.VMEM((operand, 2 * vecs, LANE), jnp.bfloat16),
            *(pltpu.VMEM(shape, jnp.float32) for shape in extra),
            pltpu.SemaphoreType.DMA((slots // CHUNK + copies,)),
        ]

    whole = (YC, *piece)
    (near,) = local(
        pieces_kernel,
        [whole],
        [SMEM] * 2 + [HBM],
        [pltpu.VMEM((ZLO, vecs, LANE), jnp.float32), pltpu.SemaphoreType.DMA((ZLO,))],
        SMALL,
    )(x, yc, own)
    other = lax.ppermute(near, ("zlo", "zhi"), [(i, ZLO * ZHI - 1 - i) for i in range(ZLO * ZHI)])
    masks = [matchings] + [
        lax.ppermute(matchings, "x", [(i, (i - step) % X) for i in range(X)])
        for step in range(1, X)
    ]
    parts, mine = local(
        columns_kernel,
        [(FAN, REGIONS - 1, *piece), (blocks, vecs, LANE)],
        [SMEM] * 3 + [HBM] * 2,
        [
            *tile_scratch(
                blocks, [(REGIONS * blocks, vecs, LANE), own.shape, (FAN, REGIONS - 1, *piece)], 1
            ),
            pltpu.SemaphoreType.DMA((X + 1,)),
        ],
        LARGE,
        half,
        HBM,
    )(*ids, tile_set, own)
    parts = exchange(parts, FAN_AXES)
    side = (Y, ZHI, *piece)
    same, cross = local(pair_kernel, [side] * CORE, [VMEM] * 2, limit=SMALL)(near, other)
    cross = lax.ppermute(cross, "core", [(0, 1), (1, 0)])
    pieces = local(join_kernel, [(CORE, ZHI, *piece)] * Y, [VMEM] * 2, limit=SMALL)(same, cross)
    pieces = swaps(pieces, "y", Y)
    (wanted,) = local(
        route_kernel,
        [(FAN, REGIONS - 1, *piece)],
        [SMEM] * 6 + [VMEM] * Y,
        [
            pltpu.VMEM((OWN, *piece), jnp.float32),
            pltpu.VMEM((FAN, REGIONS - 1, *piece), jnp.float32),
            pltpu.SemaphoreType.DMA((X,)),
        ],
        SMALL,
        place=HBM,
    )(x, yc, *masks, *pieces)
    parts, wanted = lax.optimization_barrier((parts, wanted))
    far = exchange(wanted, FAN_AXES)
    spread = (ZLO, YC, SUB, LANE)
    near, other = local(
        collect_kernel,
        [spread] * 2,
        [SMEM] * 7 + [VMEM],
        [pltpu.VMEM((ZLO, OWN, SUB, LANE), jnp.float32)],
        SMALL,
    )(x, yc, zlo, *masks, parts)
    other = lax.ppermute(other, "zhi", [(0, 1), (1, 0)])
    parts = local(add_zhi_kernel, [spread[1:]] * ZLO, [VMEM] * 2, limit=SMALL)(near, other)
    parts = swaps(parts, "zlo", ZLO)
    parts = local(add_zlo_kernel, [spread[2:]] * YC, [VMEM] * ZLO, limit=SMALL)(*parts)
    (rows,) = local(
        rows_kernel,
        [(blocks, vecs, LANE)],
        [SMEM] * 3 + [HBM] * 4,
        tile_scratch(REGIONS * blocks, [own.shape, wanted.shape], 3),
        ROWS,
        half,
    )(*ids, tile_set, own, far, mine)
    rows, *parts = lax.optimization_barrier((rows, *parts))
    rows = exchange(rows, GRP_AXES)
    parts = swaps(parts, YC_AXES, YC)
    (total,) = local(final_kernel, [(vecs, LANE)], [SMEM] + [VMEM] * (1 + YC), limit=SMALL)(
        yc, rows, *parts
    )
    return total[None]


def solution(mesh):
    fine = Mesh(mesh.devices.reshape(ZLO, X, ZHI, Y, CORE), ("zlo", "x", "zhi", "y", "core"))
    return jax.shard_map(
        on_device,
        mesh=fine,
        in_specs=(
            P(OWN_AXES, None, None),
            P(GRP_AXES, OWN_AXES, None, None, None),
            P(GRP_AXES, OWN_AXES, None),
            P(GRP_AXES, OWN_AXES, None),
            P(GRP_AXES, OWN_AXES),
            P(GRP_AXES, None),
        ),
        out_specs=P(OWN_AXES, None, GRP_AXES),
        check_vma=False,
    )
```

```python
import jax
import jax.numpy as jnp
from jax import lax
from jax.experimental import pallas as pl
from jax.experimental.pallas import tpu as pltpu
from jax.sharding import Mesh, PartitionSpec as P

ZLO, X, ZHI, Y, CORE = 4, 4, 2, 4, 2
YC = Y * CORE
OWN = ZHI * YC
FAN = X * YC
GRP_AXES = ("zlo", "x")
OWN_AXES = ("zhi", "y", "core")
FAN_AXES = ("x", "y", "core")
YC_AXES = ("y", "core")


REGIONS = 4
SUB = 8
LANE = 128
CHUNK = 32
GROUPS = (32, 8, 1)
SMALL = 8 << 20
LARGE = 56 << 20
ROWS = 52 << 20

VMEM = pl.BlockSpec(memory_space=pltpu.VMEM)
SMEM = pl.BlockSpec(memory_space=pltpu.SMEM)
HBM = pl.BlockSpec(memory_space=pltpu.HBM)

BY_COLS = (((1,), (0,)), ((), ()))
BY_ROWS = (((1,), (1,)), ((), ()))


def halves(value):
    high = value.astype(jnp.bfloat16)
    return high, (value - high.astype(jnp.float32)).astype(jnp.bfloat16)


def dot(left, right, dims):
    return lax.dot_general(left, right, dims, preferred_element_type=jnp.float32)


def by_columns(pair, high, low):
    count = pair.shape[0] // 2
    wide = dot(pair, jnp.concatenate([high, low], axis=1), BY_COLS)
    return wide[:count, :LANE] + wide[count:, :LANE] + wide[:count, LANE:]


def by_rows(pair, high, low):
    count = pair.shape[0] // 2
    top = jnp.concatenate([pair[:count], pair[:count]], axis=1)
    bottom = jnp.concatenate([pair[count:], jnp.zeros_like(pair[count:])], axis=1)
    tall = dot(
        jnp.concatenate([top, bottom], axis=0), jnp.concatenate([high, low], axis=1), BY_ROWS
    )
    return tall[:count] + tall[count:]


def pieces_kernel(x_ref, yc_ref, own_ref, out_ref, held, sems):
    copies = []
    for zlo in range(ZLO):
        col = pl.multiple_of((zlo * X + x_ref[0]) * LANE, LANE)
        copies.append(
            pltpu.make_async_copy(own_ref.at[:, pl.ds(col, LANE)], held.at[zlo], sems.at[zlo])
        )
    for copy in copies:
        copy.start()
    for copy in copies:
        copy.wait()
    for step in range(YC):
        row = pl.multiple_of((yc_ref[0] ^ step) * SUB, SUB)
        for zlo in range(ZLO):
            out_ref[step, zlo] = held[zlo, pl.ds(row, SUB)]


def pair_kernel(near_ref, other_ref, same_ref, cross_ref):
    for step in range(Y):
        for core, out_ref in enumerate((same_ref, cross_ref)):
            out_ref[step, 0] = near_ref[step * CORE + core]
            out_ref[step, 1] = other_ref[step * CORE + core]


def join_kernel(same_ref, cross_ref, *outs):
    for step in range(Y):
        outs[step][0] = same_ref[step]
        outs[step][1] = cross_ref[step]


def route_kernel(x_ref, yc_ref, m0, m1, m2, m3, *refs):
    pieces, (out, held, out_ref, sems) = refs[:Y], refs[Y:]
    for step in range(Y):
        for core in range(CORE):
            for zhi in range(ZHI):
                held[zhi * YC + step * CORE + core] = pieces[step][core, zhi]
    results = []
    for step, masks in enumerate((m0, m1, m2, m3)):
        base = lax.rem(x_ref[0] + step, X) * YC
        for slot in range(REGIONS - 1):
            mask = masks[0, slot]
            for part in range(YC):
                out_ref[base + part, slot] = held[(part ^ yc_ref[0]) ^ mask]
        here = pl.ds(base, YC)
        results.append(pltpu.make_async_copy(out_ref.at[here], out.at[here], sems.at[step]))
        results[-1].start()
    for copy in results:
        copy.wait()


def collect_kernel(x_ref, yc_ref, zlo_ref, m0, m1, m2, m3, parts_ref, near_ref, other_ref, sums):
    sums[...] = jnp.zeros_like(sums)
    for step, masks in enumerate((m0, m1, m2, m3)):
        base = lax.rem(x_ref[0] + step, X) * YC
        for slot in range(REGIONS - 1):
            mask = masks[0, slot]
            for part in range(YC):
                owner = (part ^ yc_ref[0]) ^ mask
                for zlo in range(ZLO):
                    sums[zlo, owner] += parts_ref[base + part, slot, zlo]
    for step in range(ZLO):
        zlo = zlo_ref[0] ^ step
        near_ref[step] = sums[zlo, :YC]
        other_ref[step] = sums[zlo, YC:]


def add_zhi_kernel(a_ref, b_ref, *outs):
    for step in range(ZLO):
        outs[step][...] = a_ref[step] + b_ref[step]


def add_zlo_kernel(a_ref, b_ref, c_ref, d_ref, same_ref, cross_ref):
    for step in range(Y):
        for core, out_ref in enumerate((same_ref, cross_ref)):
            at = step * CORE + core
            out_ref[step] = (a_ref[at] + b_ref[at]) + (c_ref[at] + d_ref[at])


def final_kernel(yc_ref, rows_ref, *refs):
    parts, out_ref = refs[:Y], refs[Y]
    for step in range(YC):
        at = pl.ds(pl.multiple_of((yc_ref[0] ^ step) * SUB, SUB), SUB)
        total = parts[step // CORE][step % CORE]
        for group in range(rows_ref.shape[0]):
            total = total + rows_ref[group, at]
        out_ref[at] = total


def load_table(table, base, blocks, get, vecs):
    for block in range(blocks):
        high, low = halves(get(block))
        table[base + block, :vecs] = high
        table[base + block, vecs:] = low


def fetch(tiles, held, sems):
    copies = [
        pltpu.make_async_copy(
            tiles.at[pl.ds(i * CHUNK, CHUNK)], held.at[pl.ds(i * CHUNK, CHUNK)], sems.at[i]
        )
        for i in range(held.shape[0] // CHUNK)
    ]
    for copy in copies:
        copy.start()
    return copies


def each_group(copies, live, group):
    for i, copy in enumerate(copies):
        copy.wait()
        done = 0
        here = jnp.clip(live - i * CHUNK, 0, CHUNK)
        for size in GROUPS:

            def step(at, carry, i=i, size=size):
                group(i * CHUNK + at * size, size)
                return carry

            lax.fori_loop(done // size, here // size, step, 0)
            done = here // size * size


def columns_kernel(
    rows, cols, count, tiles, own, out, self_out, held, table, sums, near, out_ref, sems, out_sems
):
    first = pltpu.make_async_copy(own, near, sems.at[sems.shape[0] - 1])
    first.start()
    copies = fetch(tiles, held, sems)
    sums[...] = jnp.zeros_like(sums)
    vecs = near.shape[0]
    blocks = near.shape[1] // LANE
    first.wait()
    load_table(table, 0, blocks, lambda b: near[:, b * LANE : (b + 1) * LANE], vecs)

    def group(first, size):
        done = []
        for k in range(size):
            done.append(by_columns(table[rows[first + k]], *halves(held[first + k])))
        for k in range(size):
            col = cols[first + k]
            sums[col] += done[k]

    each_group(copies, count[0], group)
    mine = pltpu.make_async_copy(sums.at[pl.ds(0, blocks)], self_out, out_sems.at[X])
    mine.start()
    results = []
    for x in range(X):
        here = pl.ds(x * YC, YC)
        for slot in range(REGIONS - 1):
            for zlo in range(blocks // X):
                value = sums[(slot + 1) * blocks + zlo * X + x]
                for part in range(YC):
                    out_ref[x * YC + part, slot, zlo] = value[part * SUB : (part + 1) * SUB]
        results.append(pltpu.make_async_copy(out_ref.at[here], out.at[here], out_sems.at[x]))
        results[-1].start()
    for copy in (mine, *results):
        copy.wait()


def rows_kernel(
    rows, cols, count, tiles, own, far, mine, sums, held, table, near, away, sems
):
    last = sems.shape[0] - 3
    operands = [
        pltpu.make_async_copy(source, target, sems.at[last + i])
        for i, (source, target) in enumerate(((own, near), (far, away), (mine, sums)))
    ]
    for copy in operands:
        copy.start()
    copies = fetch(tiles, held, sems)
    vecs = near.shape[0]
    blocks = near.shape[1] // LANE
    operands[0].wait()
    load_table(table, 0, blocks, lambda b: near[:, b * LANE : (b + 1) * LANE], vecs)
    operands[1].wait()
    for slot in range(REGIONS - 1):

        def piece(b, slot=slot):
            return jnp.concatenate(
                [away[b % X * YC + part, slot, b // X] for part in range(YC)], axis=0
            )

        load_table(table, (slot + 1) * blocks, blocks, piece, vecs)
    operands[2].wait()

    def group(first, size):
        done = []
        for k in range(size):
            done.append(by_rows(table[cols[first + k]], *halves(held[first + k])))
        for k in range(size):
            row = rows[first + k]
            sums[row] += done[k]

    each_group(copies, count[0], group)


def exchange(value, axes):
    return lax.all_to_all(value, axes, 0, 0, tiled=False)


def local(kernel, outs, specs, scratch=(), limit=None, cost=None, place=VMEM):
    outs = [jax.ShapeDtypeStruct(shape, jnp.float32) for shape in outs]
    return pl.pallas_call(
        kernel,
        out_shape=outs,
        in_specs=specs,
        out_specs=[place] * len(outs),
        scratch_shapes=scratch,
        compiler_params=pltpu.CompilerParams(vmem_limit_bytes=limit),
        cost_estimate=cost,
    )


def swaps(arrays, axes, count):
    return [arrays[0]] + [
        lax.ppermute(arrays[step], axes, [(i, i ^ step) for i in range(count)])
        for step in range(1, count)
    ]


def on_device(vectors, tiles, tile_rows, tile_cols, tile_counts, matchings):
    own = vectors[0]
    tile_set = tiles[0, 0]
    vecs, rows_own = own.shape
    slots = tile_set.shape[0]
    blocks = rows_own // LANE
    x, zlo, yc = (
        lax.axis_index(axes).reshape(1).astype(jnp.int32) for axes in ("x", "zlo", YC_AXES)
    )
    ids = (tile_rows[0, 0], tile_cols[0, 0], tile_counts[0])
    piece = (ZLO, SUB, LANE)
    half = pl.CostEstimate(
        flops=slots * 6 * vecs * LANE * LANE, bytes_accessed=tile_set.size * 4, transcendentals=0
    )

    def tile_scratch(operand, extra, copies):
        return [
            pltpu.VMEM(tile_set.shape, jnp.float32),
            pltpu.VMEM((operand, 2 * vecs, LANE), jnp.bfloat16),
            *(pltpu.VMEM(shape, jnp.float32) for shape in extra),
            pltpu.SemaphoreType.DMA((slots // CHUNK + copies,)),
        ]

    whole = (YC, *piece)
    (near,) = local(
        pieces_kernel,
        [whole],
        [SMEM] * 2 + [HBM],
        [pltpu.VMEM((ZLO, vecs, LANE), jnp.float32), pltpu.SemaphoreType.DMA((ZLO,))],
        SMALL,
    )(x, yc, own)
    other = lax.ppermute(near, ("zlo", "zhi"), [(i, ZLO * ZHI - 1 - i) for i in range(ZLO * ZHI)])
    masks = [matchings] + [
        lax.ppermute(matchings, "x", [(i, (i - step) % X) for i in range(X)])
        for step in range(1, X)
    ]
    parts, mine = local(
        columns_kernel,
        [(FAN, REGIONS - 1, *piece), (blocks, vecs, LANE)],
        [SMEM] * 3 + [HBM] * 2,
        [
            *tile_scratch(
                blocks, [(REGIONS * blocks, vecs, LANE), own.shape, (FAN, REGIONS - 1, *piece)], 1
            ),
            pltpu.SemaphoreType.DMA((X + 1,)),
        ],
        LARGE,
        half,
        HBM,
    )(*ids, tile_set, own)
    parts = exchange(parts, FAN_AXES)
    side = (Y, ZHI, *piece)
    same, cross = local(pair_kernel, [side] * CORE, [VMEM] * 2, limit=SMALL)(near, other)
    cross = lax.ppermute(cross, "core", [(0, 1), (1, 0)])
    pieces = local(join_kernel, [(CORE, ZHI, *piece)] * Y, [VMEM] * 2, limit=SMALL)(same, cross)
    pieces = swaps(pieces, "y", Y)
    (wanted,) = local(
        route_kernel,
        [(FAN, REGIONS - 1, *piece)],
        [SMEM] * 6 + [VMEM] * Y,
        [
            pltpu.VMEM((OWN, *piece), jnp.float32),
            pltpu.VMEM((FAN, REGIONS - 1, *piece), jnp.float32),
            pltpu.SemaphoreType.DMA((X,)),
        ],
        SMALL,
        place=HBM,
    )(x, yc, *masks, *pieces)
    parts, wanted = lax.optimization_barrier((parts, wanted))
    far = exchange(wanted, FAN_AXES)
    spread = (ZLO, YC, SUB, LANE)
    near, other = local(
        collect_kernel,
        [spread] * 2,
        [SMEM] * 7 + [VMEM],
        [pltpu.VMEM((ZLO, OWN, SUB, LANE), jnp.float32)],
        SMALL,
    )(x, yc, zlo, *masks, parts)
    other = lax.ppermute(other, "zhi", [(0, 1), (1, 0)])
    parts = local(add_zhi_kernel, [spread[1:]] * ZLO, [VMEM] * 2, limit=SMALL)(near, other)
    parts = swaps(parts, "zlo", ZLO)
    side = (Y, SUB, LANE)
    parts = local(add_zlo_kernel, [side] * CORE, [VMEM] * ZLO, limit=SMALL)(*parts)
    (rows,) = local(
        rows_kernel,
        [(blocks, vecs, LANE)],
        [SMEM] * 3 + [HBM] * 4,
        tile_scratch(REGIONS * blocks, [own.shape, wanted.shape], 3),
        ROWS,
        half,
    )(*ids, tile_set, own, far, mine)
    rows, *parts = lax.optimization_barrier((rows, *parts))
    rows = exchange(rows, GRP_AXES)
    cross = lax.ppermute(parts[1], "core", [(0, 1), (1, 0)])
    parts = local(join_kernel, [(CORE, SUB, LANE)] * Y, [VMEM] * 2, limit=SMALL)(parts[0], cross)
    parts = swaps(parts, "y", Y)
    (total,) = local(final_kernel, [(vecs, LANE)], [SMEM] + [VMEM] * (1 + Y), limit=SMALL)(
        yc, rows, *parts
    )
    return total[None]


def solution(mesh):
    fine = Mesh(mesh.devices.reshape(ZLO, X, ZHI, Y, CORE), ("zlo", "x", "zhi", "y", "core"))
    return jax.shard_map(
        on_device,
        mesh=fine,
        in_specs=(
            P(OWN_AXES, None, None),
            P(GRP_AXES, OWN_AXES, None, None, None),
            P(GRP_AXES, OWN_AXES, None),
            P(GRP_AXES, OWN_AXES, None),
            P(GRP_AXES, OWN_AXES),
            P(GRP_AXES, None),
        ),
        out_specs=P(OWN_AXES, None, GRP_AXES),
        check_vma=False,
    )
```
